32 devices in a mesh: dp: 8 (over y, x, core), tensor: 4 (over z).
Axes of the slice: x: 2, y: 2, z: 4, core: 2. Of those that a mesh axis runs over, the one named last changes fastest.
Arguments:
- block_input: bfloat16 [3072, 1024], P(('dp', 'tensor')), may hold values from -45 to 45
- positions: int32 [3072], P('dp'), may hold values from 0 to 383, as said below
- out_grad: bfloat16 [3072, 1024], P(('dp', 'tensor')), may hold values from -6 to 6
- in_gain: bfloat16 [1024], P(('tensor', 'dp')), may hold values from 0.5 to 1.5
- z_proj: bfloat16 [1024, 1536], P('dp', 'tensor'), may hold values from -0.1875 to 0.1875
- x_proj: bfloat16 [1024, 1536], P('dp', 'tensor'), may hold values from -0.1875 to 0.1875
- step_proj: bfloat16 [1024, 24], P('dp', 'tensor'), may hold values from -0.1875 to 0.1875
- state_proj: bfloat16 [1024, 256], P(('tensor', 'dp')), may hold values from -0.1875 to 0.1875
- x_conv: bfloat16 [4, 24, 64], P(None, 'tensor', 'dp'), may hold values from -3 to 3
- x_conv_bias: bfloat16 [24, 64], P('tensor', 'dp'), may hold values from -3 to 3
- state_conv: bfloat16 [4, 256], P(None, ('tensor', 'dp')), may hold values from -3 to 3
- state_conv_bias: bfloat16 [256], P(('tensor', 'dp')), may hold values from -3 to 3
- decay_log: float32 [24], P('tensor'), may hold values from -2.5 to 1.5
- step_bias: float32 [24], P('tensor'), may hold values from -4.5 to -1
- skip_gain: float32 [24], P('tensor'), may hold values from -3 to 3
- mixer_gain: bfloat16 [24, 64], P('tensor', 'dp'), may hold values from 0.5 to 1.5
- mixer_out: bfloat16 [1536, 1024], P('tensor', 'dp'), may hold values from -0.15625 to 0.15625
- query_proj: bfloat16 [1024, 1024], P('dp', 'tensor'), may hold values from -0.1875 to 0.1875
- keyval_proj: bfloat16 [1024, 512], P(('tensor', 'dp')), may hold values from -0.1875 to 0.1875
- attn_out: bfloat16 [1024, 1024], P('tensor', 'dp'), may hold values from -0.75 to 0.75
- ffn_gain: bfloat16 [1024], P(('tensor', 'dp')), may hold values from 0.5 to 1.5
- gate_proj: bfloat16 [1024, 2048], P('dp', 'tensor'), may hold values from -0.1875 to 0.1875
- up_proj: bfloat16 [1024, 2048], P('dp', 'tensor'), may hold values from -0.1875 to 0.1875
- down_proj: bfloat16 [2048, 1024], P('tensor', 'dp'), may hold values from -0.125 to 0.125
Outputs:
- output: bfloat16 [3072, 1024], P(('dp', 'tensor'))
- input_grad: float32 [3072, 1024], P(('dp', 'tensor'))
- in_gain_grad: float32 [1024], P(('tensor', 'dp'))
- z_proj_grad: float32 [1024, 1536], P('dp', 'tensor')
- x_proj_grad: float32 [1024, 1536], P('dp', 'tensor')
- step_proj_grad: float32 [1024, 24], P('dp', 'tensor')
- state_proj_grad: float32 [1024, 256], P(('tensor', 'dp'))
- x_conv_grad: float32 [4, 24, 64], P(None, 'tensor', 'dp')
- x_conv_bias_grad: float32 [24, 64], P('tensor', 'dp')
- state_conv_grad: float32 [4, 256], P(None, ('tensor', 'dp'))
- state_conv_bias_grad: float32 [256], P(('tensor', 'dp'))
- decay_log_grad: float32 [24], P('tensor')
- step_bias_grad: float32 [24], P('tensor')
- skip_gain_grad: float32 [24], P('tensor')
- mixer_gain_grad: float32 [24, 64], P('tensor', 'dp')
- mixer_out_grad: float32 [1536, 1024], P('tensor', 'dp')
- query_proj_grad: float32 [1024, 1024], P('dp', 'tensor')
- keyval_proj_grad: float32 [1024, 512], P(('tensor', 'dp'))
- attn_out_grad: float32 [1024, 1024], P('tensor', 'dp')
- ffn_gain_grad: float32 [1024], P(('tensor', 'dp'))
- gate_proj_grad: float32 [1024, 2048], P('dp', 'tensor')
- up_proj_grad: float32 [1024, 2048], P('dp', 'tensor')
- down_proj_grad: float32 [2048, 1024], P('tensor', 'dp')
The draws below stay inside these ranges and needn't reach their ends.
Inputs may be any that keep to these rules, and one draw needn't show every extreme that they name: `positions`: each aligned block of 384 entries (one data group's tokens) holds whole sequences one after another: an entry is 0 where a sequence begins, always so at a block's first entry, and one more than the entry before it otherwise. In every draw some block holds a single sequence of 384 tokens.
All inputs are finite; a program needn't handle non-finite values.
Results may differ from the reference program's by a relative error of at most 0.03.
Values may be sent and summed in bfloat16 or wider, within the bound.
No kernel may reach another device: no remote copies, remote signals or barrier semaphores. Data moves between devices by JAX's collectives and lax.ppermute only.
A program may use at most 128 MiB of HBM per device.

```python
import jax
import jax.numpy as jnp
from jax import lax

D = 1024
FF = 2048
H = 24
HD = 64
NSTATE = 128
KCONV = 4
QH = 8
KVH = 2
AHD = 128
R = 384
DS = 1536
TOKENS = 3072


def draw_block_input(key, part):
    key_noise, key_rows, key_cols = jax.random.split(key, 3)
    noise = jax.random.truncated_normal(key_noise, -4.0, 4.0, (TOKENS, D), jnp.float32)
    row_scale = jnp.exp(jax.random.uniform(key_rows, (TOKENS, 1), jnp.float32, -1.2, 1.2))
    col_scale = jnp.exp(jax.random.uniform(key_cols, (1, D), jnp.float32, -1.2, 1.2))
    return (noise * row_scale * col_scale).astype(jnp.bfloat16)


def draw_positions(key, part):
    groups = TOKENS // R
    key_level, key_flag, key_full = jax.random.split(key, 3)
    levels = jax.random.randint(key_level, (groups, 1), 1, 10)
    limits = jnp.left_shift(jnp.ones((groups, 1), jnp.int32), levels)
    start_flags = jax.random.randint(key_flag, (groups, R), 0, limits) == 0
    full_group = jax.random.randint(key_full, (), 0, groups)
    group_index = jnp.arange(groups)[:, None]
    slot_index = jnp.arange(R)[None, :]
    starts = start_flags & (group_index != full_group) | (slot_index == 0)
    last_start = lax.cummax(jnp.where(starts, slot_index, 0), axis=1)
    return (slot_index - last_start).reshape(TOKENS).astype(jnp.int32)


def steps_of(stream_key, extent, cuts, least, high):
    def one(axis_at, blocks):
        heights = jax.random.uniform(jax.random.fold_in(jax.random.fold_in(stream_key, 6), axis_at), (blocks,), jnp.float32, least / len(cuts), high / len(cuts))
        return jnp.repeat(jnp.exp(heights), extent[axis_at] // blocks).reshape((-1,) + (1,) * (len(extent) - axis_at - 1))

    loudness = one(*cuts[0])
    for cut in cuts[1:]:
        loudness = loudness * one(*cut)
    return loudness


def centred(stream_key, extent, spread, reach, cuts=(), kind=jnp.bfloat16):
    factor_of = steps_of(stream_key, extent, cuts, -0.22, 0.18) if cuts else 1.0
    result = jax.random.normal(stream_key, extent, jnp.float32) * spread * factor_of
    return jnp.minimum(jnp.maximum(result, -reach), reach).astype(kind)


def setup_inputs(seed: int = 0) -> dict:
    key_list = jax.random.split(jax.random.key(seed), 25)
    block_input = draw_block_input(jax.random.fold_in(key_list[24], 71), 0)
    positions = draw_positions(jax.random.fold_in(key_list[24], 71), 0)
    out_grad = centred(key_list[2], (TOKENS, D), 1.0, 6.0, ((0, 32),))
    in_gain = jnp.clip(1.0 + 0.1 * jax.random.normal(key_list[3], (D,), jnp.float32), 0.5, 1.5).astype(jnp.bfloat16)
    z_proj = centred(key_list[4], (D, DS), D ** -0.5, 0.1875, ((0, 8), (1, 4)))
    x_proj = centred(key_list[5], (D, DS), D ** -0.5, 0.1875, ((0, 8), (1, 4)))
    step_proj = centred(key_list[6], (D, H), D ** -0.5, 0.1875, ((0, 8), (1, 4)))
    state_proj = centred(key_list[7], (D, 2 * NSTATE), D ** -0.5, 0.1875, ((0, 32),))
    x_conv = centred(key_list[8], (KCONV, H, HD), 0.5, 3.0, ((1, 4), (2, 8)))
    x_conv_bias = centred(key_list[9], (H, HD), 0.5, 3.0, ((0, 4), (1, 8)))
    state_conv = centred(key_list[10], (KCONV, 2 * NSTATE), 0.5, 3.0, ((1, 32),))
    state_conv_bias = centred(key_list[11], (2 * NSTATE,), 0.5, 3.0, ((0, 32),))
    decay_log = jnp.clip(-2.5 + 4.0 * jax.random.uniform(key_list[12], (H,), jnp.float32) ** steps_of(key_list[12], (H,), ((0, 4),), -0.2, 0.2), -2.5, 1.5)
    step_bias = jnp.clip(-4.5 + 3.5 * jax.random.uniform(key_list[13], (H,), jnp.float32) ** steps_of(key_list[13], (H,), ((0, 4),), -0.2, 0.2), -4.5, -1.0)
    skip_gain = centred(key_list[14], (H,), 1.0, 3.0, ((0, 4),), jnp.float32)
    mixer_gain = jnp.clip(1.0 + 0.1 * jax.random.normal(key_list[15], (H, HD), jnp.float32), 0.5, 1.5).astype(jnp.bfloat16)
    mixer_out = centred(key_list[16], (DS, D), DS ** -0.5, 0.15625, ((0, 4), (1, 8)))
    query_proj = centred(key_list[17], (D, QH * AHD), D ** -0.5, 0.1875, ((0, 8), (1, 4)))
    keyval_proj = centred(key_list[18], (D, 2 * KVH * AHD), D ** -0.5, 0.1875, ((0, 32),))
    attn_out = centred(key_list[19], (QH * AHD, D), (QH * AHD // 16) ** -0.5, 0.75, ((0, 4), (1, 8)))
    ffn_gain = jnp.clip(1.0 + 0.1 * jax.random.normal(key_list[20], (D,), jnp.float32), 0.5, 1.5).astype(jnp.bfloat16)
    gate_proj = centred(key_list[21], (D, FF), D ** -0.5, 0.1875, ((0, 8), (1, 4)))
    up_proj = centred(key_list[22], (D, FF), D ** -0.5, 0.1875, ((0, 8), (1, 4)))
    down_proj = centred(key_list[23], (FF, D), FF ** -0.5, 0.125, ((0, 4), (1, 8)))
    return {"block_input": block_input, "positions": positions, "out_grad": out_grad, "in_gain": in_gain, "z_proj": z_proj, "x_proj": x_proj, "step_proj": step_proj, "state_proj": state_proj, "x_conv": x_conv, "x_conv_bias": x_conv_bias, "state_conv": state_conv, "state_conv_bias": state_conv_bias, "decay_log": decay_log, "step_bias": step_bias, "skip_gain": skip_gain, "mixer_gain": mixer_gain, "mixer_out": mixer_out, "query_proj": query_proj, "keyval_proj": keyval_proj, "attn_out": attn_out, "ffn_gain": ffn_gain, "gate_proj": gate_proj, "up_proj": up_proj, "down_proj": down_proj}


norm_eps = 1e-05
rope_base = 10000.0

def matmul(left, right):
    return jnp.dot(left, right, preferred_element_type=jnp.float32)

def to_half(pre_values):
    return lax.optimization_barrier(pre_values.astype(jnp.bfloat16))

def silu_grad(pre_values):
    sigmoid_part = jax.nn.sigmoid(pre_values)
    return sigmoid_part * (1.0 + pre_values * (1.0 - sigmoid_part))

def causal_conv(inputs, tap_weights, bias_row, positions):
    row_count = inputs.shape[0]
    running = jnp.zeros_like(inputs) + bias_row.astype(jnp.float32)[None, :]
    for tap_index in range(tap_weights.shape[0]):
        shifted = jnp.pad(inputs, ((tap_index, 0), (0, 0)))[:row_count]
        allowed = (positions >= tap_index).astype(jnp.float32)[:, None]
        running = running + tap_weights[tap_index].astype(jnp.float32)[None, :] * shifted * allowed
    return running

def conv_backward(grad_pre, inputs, tap_weights, positions):
    row_count = inputs.shape[0]
    tap_grads = []
    grad_inputs = jnp.zeros_like(inputs)
    for tap_index in range(tap_weights.shape[0]):
        allowed = (positions >= tap_index).astype(jnp.float32)[:, None]
        masked = grad_pre * allowed
        shifted = jnp.pad(inputs, ((tap_index, 0), (0, 0)))[:row_count]
        tap_grads.append(lax.optimization_barrier(jnp.sum(masked * shifted, axis=0)))
        moved_back = jnp.pad(masked, ((0, tap_index), (0, 0)))[tap_index:]
        grad_inputs = grad_inputs + tap_weights[tap_index].astype(jnp.float32)[None, :] * moved_back
    return (jnp.stack(tap_grads), lax.optimization_barrier(jnp.sum(grad_pre, axis=0)), grad_inputs)

def segment_mask(positions):
    row_count = positions.shape[0]
    query_index = jnp.arange(row_count)[:, None]
    key_index = jnp.arange(row_count)[None, :]
    return (key_index <= query_index) & (key_index >= query_index - positions[:, None])

def rope_tables(positions, width):
    half_width = width // 2
    freq_rates = rope_base ** (-2.0 * jnp.arange(half_width, dtype=jnp.float32) / width)
    angles = positions.astype(jnp.float32)[:, None] * freq_rates[None, :]
    return (jnp.cos(angles), jnp.sin(angles))

def rotate(pre_values, cosine, sine_table):
    half_width = pre_values.shape[-1] // 2
    first_half = pre_values[..., :half_width]
    second_half = pre_values[..., half_width:]
    cos_rows = cosine[:, None, :]
    sin_rows = sine_table[:, None, :]
    return jnp.concatenate([first_half * cos_rows - second_half * sin_rows, second_half * cos_rows + first_half * sin_rows], axis=-1)

def rotate_back(grad_values, cosine, sine_table):
    half_width = grad_values.shape[-1] // 2
    first_half = grad_values[..., :half_width]
    second_half = grad_values[..., half_width:]
    cos_rows = cosine[:, None, :]
    sin_rows = sine_table[:, None, :]
    return jnp.concatenate([first_half * cos_rows + second_half * sin_rows, second_half * cos_rows - first_half * sin_rows], axis=-1)

def layer_group(rows_in, positions, grad_rows, params):
    in_gain, z_proj, x_proj, step_proj, state_proj, x_conv, x_conv_bias, state_conv, state_conv_bias, decay_log, step_bias, skip_gain, mixer_gain, mixer_out, query_proj, keyval_proj, attn_out, ffn_gain, gate_proj, up_proj, down_proj = params
    row_count = rows_in.shape[0]
    group_size = QH // KVH
    resid_in = rows_in.astype(jnp.float32)
    in_scale = lax.rsqrt(lax.optimization_barrier(jnp.mean(resid_in * resid_in, axis=1, keepdims=True)) + norm_eps)
    in_gain_f = in_gain.astype(jnp.float32)
    normed = to_half(resid_in * in_scale * in_gain_f[None, :])
    gate_z = matmul(normed, z_proj)
    x_lin = matmul(normed, x_proj)
    step_raw = matmul(normed, step_proj)
    state_lin = matmul(normed, state_proj)
    x_taps = x_conv.reshape(KCONV, DS)
    x_pre = causal_conv(x_lin, x_taps, x_conv_bias.reshape(DS), positions)
    x_act = jax.nn.silu(x_pre)
    state_pre = causal_conv(state_lin, state_conv, state_conv_bias, positions)
    state_act = jax.nn.silu(state_pre)
    b_matrix = to_half(state_act[:, :NSTATE])
    c_matrix = to_half(state_act[:, NSTATE:])
    step_size = jax.nn.softplus(step_raw + step_bias[None, :])
    decay_rate = -jnp.exp(decay_log)
    cum_decay = jnp.cumsum(step_size * decay_rate[None, :], axis=0)
    cum_heads = cum_decay.T
    seg_mask = segment_mask(positions)
    decay_mat = jnp.exp(jnp.where(seg_mask[None], cum_heads[:, :, None] - cum_heads[:, None, :], -jnp.inf))
    gram_mat = matmul(c_matrix, b_matrix.T)
    mix_mat = to_half(decay_mat * gram_mat[None])
    x_heads = x_act.reshape(row_count, H, HD)
    drive_in = to_half(step_size[:, :, None] * x_heads)
    ssm_out = jnp.einsum('hts,shp->thp', mix_mat.astype(jnp.float32), drive_in.astype(jnp.float32)) + skip_gain[None, :, None] * x_heads
    ssm_flat = ssm_out.reshape(row_count, DS)
    gate_silu = jax.nn.silu(gate_z)
    gated_out = ssm_flat * gate_silu
    ssm_scale = lax.rsqrt(lax.optimization_barrier(jnp.mean(gated_out * gated_out, axis=1, keepdims=True)) + norm_eps)
    mixer_gain_f = mixer_gain.reshape(DS).astype(jnp.float32)
    ssm_normed = to_half(gated_out * ssm_scale * mixer_gain_f[None, :])
    query_lin = matmul(normed, query_proj).reshape(row_count, QH, AHD)
    keyval_lin = matmul(normed, keyval_proj)
    key_lin = keyval_lin[:, :KVH * AHD].reshape(row_count, KVH, AHD)
    value_lin = keyval_lin[:, KVH * AHD:].reshape(row_count, KVH, AHD)
    cosine, sine_table = rope_tables(positions, AHD)
    query_rot = to_half(rotate(query_lin, cosine, sine_table))
    key_rot = jnp.repeat(to_half(rotate(key_lin, cosine, sine_table)), group_size, axis=1)
    value_rep = jnp.repeat(to_half(value_lin), group_size, axis=1)
    score_scale = AHD ** (-0.5)
    scores = jnp.einsum('thd,shd->hts', query_rot.astype(jnp.float32), key_rot.astype(jnp.float32)) * score_scale
    exp_scores = jnp.exp(jnp.where(seg_mask[None], scores, -jnp.inf))
    row_totals = lax.optimization_barrier(jnp.sum(exp_scores, axis=2, keepdims=True))
    log_total = jnp.log(row_totals)
    attn_prob = to_half(exp_scores / row_totals)
    context = to_half(jnp.einsum('hts,shd->thd', attn_prob.astype(jnp.float32), value_rep.astype(jnp.float32))).reshape(row_count, QH * AHD)
    hidden = resid_in + (matmul(ssm_normed, mixer_out) + matmul(context, attn_out))
    ff_scale = lax.rsqrt(lax.optimization_barrier(jnp.mean(hidden * hidden, axis=1, keepdims=True)) + norm_eps)
    ffn_gain_f = ffn_gain.astype(jnp.float32)
    ffn_in = to_half(hidden * ff_scale * ffn_gain_f[None, :])
    gate_lin = matmul(ffn_in, gate_proj)
    up_lin = matmul(ffn_in, up_proj)
    gate_act = jax.nn.silu(gate_lin)
    ffn_act = to_half(gate_act * up_lin)
    output = (hidden + matmul(ffn_act, down_proj)).astype(jnp.bfloat16)
    down_grad = matmul(ffn_act.T, grad_rows)
    act_grad = matmul(grad_rows, down_proj.T)
    gate_back = to_half(act_grad * up_lin * silu_grad(gate_lin))
    up_back = to_half(act_grad * gate_act)
    gate_grad = matmul(ffn_in.T, gate_back)
    up_grad = matmul(ffn_in.T, up_back)
    ffn_back = matmul(gate_back, gate_proj.T) + matmul(up_back, up_proj.T)
    ffn_gain_grad = lax.optimization_barrier(jnp.sum(ffn_back * hidden * ff_scale, axis=0))
    ffn_norm_back = ffn_back * ffn_gain_f[None, :]
    resid_grad = grad_rows.astype(jnp.float32) + ff_scale * ffn_norm_back - hidden * ff_scale ** 3 * lax.optimization_barrier(jnp.mean(ffn_norm_back * hidden, axis=1, keepdims=True))
    resid_half = to_half(resid_grad)
    mixer_grad = matmul(ssm_normed.T, resid_half)
    attn_grad = matmul(context.T, resid_half)
    ssm_back = matmul(resid_half, mixer_out.T)
    ctx_back = to_half(matmul(resid_half, attn_out.T)).reshape(row_count, QH, AHD)
    attn_back_prob = jnp.exp(jnp.where(seg_mask[None], scores - log_total, -jnp.inf))
    prob_half = to_half(attn_back_prob)
    value_grad = to_half(jnp.einsum('hts,thd->shd', prob_half.astype(jnp.float32), ctx_back.astype(jnp.float32)))
    prob_grad = jnp.einsum('thd,shd->hts', ctx_back.astype(jnp.float32), value_rep.astype(jnp.float32))
    row_delta = lax.optimization_barrier(jnp.sum(attn_back_prob * prob_grad, axis=2, keepdims=True))
    score_back = to_half(attn_back_prob * (prob_grad - row_delta) * score_scale)
    query_back = jnp.einsum('hts,shd->thd', score_back.astype(jnp.float32), key_rot.astype(jnp.float32))
    key_back = jnp.einsum('hts,thd->shd', score_back.astype(jnp.float32), query_rot.astype(jnp.float32))
    query_grad = to_half(rotate_back(query_back, cosine, sine_table)).reshape(row_count, QH * AHD)
    key_grad = to_half(rotate_back(key_back, cosine, sine_table)).reshape(row_count, QH * AHD)
    value_flat = value_grad.reshape(row_count, QH * AHD)
    query_w_grad = matmul(normed.T, query_grad)
    key_w_grad = matmul(normed.T, key_grad).reshape(D, KVH, group_size, AHD).sum(axis=2).reshape(D, KVH * AHD)
    value_w_grad = matmul(normed.T, value_flat).reshape(D, KVH, group_size, AHD).sum(axis=2).reshape(D, KVH * AHD)
    keyval_grad = jnp.concatenate([key_w_grad, value_w_grad], axis=1)
    key_tiles = jnp.repeat(keyval_proj[:, :KVH * AHD].reshape(D, KVH, AHD), group_size, axis=1).reshape(D, QH * AHD)
    value_tiles = jnp.repeat(keyval_proj[:, KVH * AHD:].reshape(D, KVH, AHD), group_size, axis=1).reshape(D, QH * AHD)
    mixer_gain_grad = lax.optimization_barrier(jnp.sum(ssm_back * gated_out * ssm_scale, axis=0)).reshape(H, HD)
    gain_back = ssm_back * mixer_gain_f[None, :]
    row_dots = lax.optimization_barrier(jnp.sum(gain_back * gated_out, axis=1, keepdims=True))
    gated_back = ssm_scale * gain_back - gated_out * ssm_scale ** 3 * row_dots / DS
    out_back = (gated_back * gate_silu).reshape(row_count, H, HD)
    z_back = to_half(gated_back * ssm_flat * silu_grad(gate_z))
    skip_grad = lax.optimization_barrier(jnp.sum(out_back * x_heads, axis=(0, 2)))
    out_half = to_half(out_back)
    drive_back = jnp.einsum('hts,thp->shp', mix_mat.astype(jnp.float32), out_half.astype(jnp.float32))
    mix_back = jnp.einsum('thp,shp->hts', out_half.astype(jnp.float32), drive_in.astype(jnp.float32))
    gram_back = lax.optimization_barrier(jnp.sum(mix_back * decay_mat, axis=0))
    pair_term = mix_back * gram_mat[None] * decay_mat
    cum_back = (lax.optimization_barrier(jnp.sum(pair_term, axis=2)) - lax.optimization_barrier(jnp.sum(pair_term, axis=1))).T
    log_decay_back = jnp.flip(jnp.cumsum(jnp.flip(cum_back, 0), axis=0), 0)
    c_back = jnp.dot(gram_back, b_matrix.astype(jnp.float32), precision=lax.Precision.HIGHEST)
    b_back = jnp.dot(gram_back.T, c_matrix.astype(jnp.float32), precision=lax.Precision.HIGHEST)
    x_act_back = skip_gain[None, :, None] * out_back + step_size[:, :, None] * drive_back
    step_raw_back = (lax.optimization_barrier(jnp.sum(drive_back * x_heads, axis=2)) + log_decay_back * decay_rate[None, :]) * jax.nn.sigmoid(step_raw + step_bias[None, :])
    step_bias_grad = lax.optimization_barrier(jnp.sum(step_raw_back, axis=0))
    decay_log_grad = lax.optimization_barrier(jnp.sum(log_decay_back * step_size, axis=0)) * decay_rate
    x_pre_back = x_act_back.reshape(row_count, DS) * silu_grad(x_pre)
    x_taps_grad, x_bias_grad, x_lin_back = conv_backward(x_pre_back, x_lin, x_taps, positions)
    state_pre_back = jnp.concatenate([b_back, c_back], axis=1) * silu_grad(state_pre)
    state_taps_grad, state_bias_grad, state_lin_back = conv_backward(state_pre_back, state_lin, state_conv, positions)
    x_lin_half = to_half(x_lin_back)
    step_raw_half = to_half(step_raw_back)
    z_grad = matmul(normed.T, z_back)
    x_grad = matmul(normed.T, x_lin_half)
    step_grad = matmul(normed.T, step_raw_half)
    state_grad = jnp.dot(normed.astype(jnp.float32).T, state_lin_back, precision=lax.Precision.HIGHEST)
    normed_back = matmul(z_back, z_proj.T) + matmul(x_lin_half, x_proj.T) + matmul(step_raw_half, step_proj.T) + jnp.dot(state_lin_back, state_proj.astype(jnp.float32).T, precision=lax.Precision.HIGHEST) + matmul(query_grad, query_proj.T) + matmul(key_grad, key_tiles.T) + matmul(value_flat, value_tiles.T)
    in_gain_grad = lax.optimization_barrier(jnp.sum(normed_back * resid_in * in_scale, axis=0))
    in_back = normed_back * in_gain_f[None, :]
    input_grad = resid_grad + in_scale * in_back - resid_in * in_scale ** 3 * lax.optimization_barrier(jnp.mean(in_back * resid_in, axis=1, keepdims=True))
    grads = (in_gain_grad, z_grad, x_grad, step_grad, state_grad, x_taps_grad.reshape(KCONV, H, HD), x_bias_grad.reshape(H, HD), state_taps_grad, state_bias_grad, decay_log_grad, step_bias_grad, skip_grad, mixer_gain_grad, mixer_grad, query_w_grad, keyval_grad, attn_grad, ffn_gain_grad, gate_grad, up_grad, down_grad)
    return (output, input_grad, grads)

def reference(block_input, positions, out_grad, in_gain, z_proj, x_proj, step_proj, state_proj, x_conv, x_conv_bias, state_conv, state_conv_bias, decay_log, step_bias, skip_gain, mixer_gain, mixer_out, query_proj, keyval_proj, attn_out, ffn_gain, gate_proj, up_proj, down_proj):
    params = (in_gain, z_proj, x_proj, step_proj, state_proj, x_conv, x_conv_bias, state_conv, state_conv_bias, decay_log, step_bias, skip_gain, mixer_gain, mixer_out, query_proj, keyval_proj, attn_out, ffn_gain, gate_proj, up_proj, down_proj)
    groups = TOKENS // R
    rows_grouped = block_input.reshape(groups, R, D)
    pos_grouped = positions.reshape(groups, R)
    grad_grouped = out_grad.reshape(groups, R, D)
    zero_grads = tuple((jnp.zeros(weight_item.shape, jnp.float32) for weight_item in params))

    def scan_step(carried, group_data):
        rows_in, group_pos, grad_rows = group_data
        out_rows, in_grad_rows, fresh_grads = layer_group(rows_in, group_pos, grad_rows, params)
        summed = tuple((older + fresh_grad for older, fresh_grad in zip(carried, fresh_grads)))
        return (summed, (out_rows, in_grad_rows))
    totals, stacked = lax.scan(scan_step, zero_grads, (rows_grouped, pos_grouped, grad_grouped))
    in_gain_grad, z_grad, x_grad, step_grad, state_grad, x_taps_grad, x_bias_grad, state_taps_grad, state_bias_grad, decay_log_grad, step_bias_grad, skip_grad, mixer_gain_grad, mixer_grad, query_w_grad, keyval_grad, attn_grad, ffn_gain_grad, gate_grad, up_grad, down_grad = totals
    output = stacked[0].reshape(TOKENS, D)
    input_grad = stacked[1].reshape(TOKENS, D)
    return (output, input_grad, in_gain_grad, z_grad, x_grad, step_grad, state_grad, x_taps_grad, x_bias_grad, state_taps_grad, state_bias_grad, decay_log_grad, step_bias_grad, skip_grad, mixer_gain_grad, mixer_grad, query_w_grad, keyval_grad, attn_grad, ffn_gain_grad, gate_grad, up_grad, down_grad)
```

```python
import jax
import jax.numpy as jnp
from jax import lax
from jax.sharding import PartitionSpec as P

HD = 64
NSTATE = 128
KVH = 2
AHD = 128

norm_eps = 1e-05
rope_base = 10000.0
bf16 = jnp.bfloat16
f32 = jnp.float32
HIGHEST = lax.Precision.HIGHEST


def dot(left, right):
    return jnp.dot(left, right, preferred_element_type=f32)


def dot_nt(left, right):
    return lax.dot_general(left, right, (((1,), (1,)), ((), ())), preferred_element_type=f32)


def dot_tn(left, right):
    return lax.dot_general(left, right, (((0,), (0,)), ((), ())), preferred_element_type=f32)


def silu_grad(pre_values):
    sigmoid_part = jax.nn.sigmoid(pre_values)
    return sigmoid_part * (1.0 + pre_values * (1.0 - sigmoid_part))


def shifted_rows(inputs, count):
    return jnp.pad(inputs, ((count, 0), (0, 0)))[: inputs.shape[0]]


def causal_conv(inputs, taps, bias_row, allowed):
    running = bias_row[None, :] + taps[0][None, :] * inputs
    for tap in range(1, taps.shape[0]):
        running = running + taps[tap][None, :] * shifted_rows(inputs, tap) * allowed[tap]
    return running


def conv_backward(grad_pre, inputs, taps, allowed):
    tap_grads = []
    grad_inputs = jnp.zeros_like(inputs)
    for tap in range(taps.shape[0]):
        masked = grad_pre * allowed[tap] if tap else grad_pre
        tap_grads.append(jnp.sum(masked * shifted_rows(inputs, tap), axis=0))
        moved_back = jnp.pad(masked, ((0, tap), (0, 0)))[tap:]
        grad_inputs = grad_inputs + taps[tap][None, :] * moved_back
    return jnp.stack(tap_grads), jnp.sum(grad_pre, axis=0), grad_inputs


def rotate(values, cosine, sine, sign):
    half = values.shape[-1] // 2
    first, second = values[..., :half], values[..., half:]
    return jnp.concatenate(
        [first * cosine - sign * second * sine, second * cosine + sign * first * sine], axis=-1
    )


class Ring:
    def __init__(self):
        self.count = lax.axis_size("dp")
        self.me = lax.axis_index("dp")
        bits = []
        bit = 2
        while bit < self.count:
            bits.append(bit)
            bit *= 2
        self.high_first = bits[::-1]
        self.orders = (bits, bits[::-1])

    def swap(self, value, bit):
        return lax.ppermute(value, "dp", [(i, i ^ bit) for i in range(self.count)])

    def rank_at(self, place):
        half = self.count // 2
        return self.me ^ ((place % half) * 2 + place // half)

    def gather(self, shard, kind):
        have = []
        value = shard
        lead = 0
        first = None
        for bit in self.orders[kind]:
            axis = sum(1 for other in have if other > bit)
            got = self.swap(value, bit)
            first = got if first is None else first
            value = jnp.stack([value, got], axis=axis)
            have.append(bit)
            lead += 1
        value = jnp.stack([value, self.swap(value, 1)], axis=0)
        return value.reshape((self.count * shard.shape[0],) + shard.shape[1:]), first

    def reduce(self, value, kind):
        wire = value.dtype
        levels = len(self.high_first)
        rest = (value.shape[0] // self.count,) + value.shape[1:]
        value = value.reshape((2,) * (levels + 1) + rest)
        total = value[0].astype(f32) + self.swap(value[1], 1).astype(f32)
        left = list(self.high_first)
        for bit in self.orders[1 - kind]:
            axis = left.index(bit)
            keep = lax.index_in_dim(total, 0, axis, keepdims=False)
            send = lax.index_in_dim(total, 1, axis, keepdims=False).astype(wire)
            total = keep + self.swap(send, bit).astype(f32)
            left.remove(bit)
        return total


def turn(value, step):
    count = lax.axis_size("tensor")
    return lax.ppermute(value, "tensor", [(i, (i + step) % count) for i in range(count)])


def z_sum(value):
    total = value
    for step in range(1, lax.axis_size("tensor")):
        total = total + turn(value, step)
    return total


def z_scatter(value):
    count = lax.axis_size("tensor")
    rank = lax.axis_index("tensor")
    blocks = value.reshape((count, value.shape[0] // count) + value.shape[1:])

    def block(step):
        return lax.dynamic_index_in_dim(blocks, (rank + step) % count, 0, keepdims=False)

    got = [turn(block(step), step) for step in range(1, count)]
    total = block(0).astype(f32)
    for part in got:
        total = total + part.astype(f32)
    return total


def z_gather_async(value):
    count = lax.axis_size("tensor")
    rank = lax.axis_index("tensor")
    whole = jnp.zeros((count,) + value.shape, value.dtype)
    whole = lax.dynamic_update_index_in_dim(whole, value, rank, 0)
    for step in range(1, count):
        whole = lax.dynamic_update_index_in_dim(
            whole, turn(value, step), (rank - step) % count, 0
        )
    return whole.reshape((count * value.shape[0],) + value.shape[1:])


def z_gather(value):
    return lax.all_gather(value, "tensor", axis=0, tiled=True)


def local(
    block_input,
    positions,
    out_grad,
    in_gain,
    z_proj,
    x_proj,
    step_proj,
    state_proj,
    x_conv,
    x_conv_bias,
    state_conv,
    state_conv_bias,
    decay_log,
    step_bias,
    skip_gain,
    mixer_gain,
    mixer_out,
    query_proj,
    keyval_proj,
    attn_out,
    ffn_gain,
    gate_proj,
    up_proj,
    down_proj,
):
    ring = Ring()
    n = ring.count
    tensor = lax.axis_size("tensor")
    rank = lax.axis_index("tensor")
    width = block_input.shape[1]
    own_rows = block_input.shape[0]
    rows = own_rows * tensor
    heads = decay_log.shape[0]
    channels = heads * HD
    all_channels = channels * tensor
    shard = width // n
    piece = width // (n * tensor)
    kcount = x_conv.shape[0]
    q_local = query_proj.shape[1] // AHD
    group_size = q_local * tensor // KVH
    kv_head = rank * q_local // group_size
    state_width = 2 * NSTATE

    step_pad = (-heads) % 128
    wzq, first_a = ring.gather(jnp.concatenate([z_proj, query_proj], axis=1), 0)
    wxs, first_b = ring.gather(
        jnp.concatenate([x_proj, jnp.pad(step_proj, ((0, 0), (0, step_pad)))], axis=1), 1
    )
    rows_nat = z_gather_async(block_input)

    small = [x_conv, x_conv_bias, mixer_gain, in_gain, ffn_gain, state_conv, state_conv_bias]
    small_sizes = [item.size for item in small]
    small_flat = jnp.concatenate([item.reshape(-1) for item in small])
    pack_width = state_width + keyval_proj.shape[1]
    small_flat = jnp.pad(small_flat, (0, (-small_flat.size) % pack_width)).reshape(-1, pack_width)
    joined = jnp.concatenate(
        [jnp.concatenate([state_proj, keyval_proj], axis=1), small_flat], axis=0
    )
    joined = lax.all_gather(joined, "tensor", axis=0)
    shared = joined[:, :piece].reshape(shard, pack_width)
    smalls = lax.all_gather(joined[:, piece:].reshape(tensor, -1), "dp", axis=0)
    smalls = smalls.transpose(1, 0, 2)
    state_rows = shared[:, :state_width]
    key_rows = lax.dynamic_slice_in_dim(shared, state_width + kv_head * AHD, AHD, 1)
    value_rows = lax.dynamic_slice_in_dim(
        shared, state_width + KVH * AHD + kv_head * AHD, AHD, 1
    )
    wst_g, _ = ring.gather(state_rows, 1)
    wkv_g, _ = ring.gather(jnp.concatenate([key_rows, value_rows], axis=1), 0)

    late = lax.optimization_barrier(
        (mixer_out.T, attn_out.T, gate_proj, up_proj, down_proj.T, first_a, first_b)
    )
    w_mix, first_c = ring.gather(late[0], 0)
    w_attn, _ = ring.gather(late[1], 0)
    w_up, first_d = ring.gather(late[3], 1)
    w_gate, _ = ring.gather(late[2], 0)
    w_down, _ = ring.gather(late[4], 1)

    offsets = [0]
    for size in small_sizes:
        offsets.append(offsets[-1] + size)

    def small_part(index):
        return smalls[:, :, offsets[index] : offsets[index + 1]]

    def own_small(index, lead):
        mine = lax.dynamic_index_in_dim(small_part(index), rank, 0, keepdims=False)
        inner = HD // n
        return (
            mine.reshape(n, lead, inner).transpose(1, 0, 2).reshape(lead, HD).astype(f32)
        )

    x_taps = own_small(0, kcount * heads).reshape(kcount, channels)
    x_bias = own_small(1, heads).reshape(channels)
    mixer_gain_f = own_small(2, heads).reshape(channels)
    in_gain_f = small_part(3).reshape(width).astype(f32)
    ffn_gain_nat = small_part(4).reshape(width)
    state_inner = state_width // (n * tensor)
    state_taps = (
        small_part(5)
        .reshape(tensor, n, kcount, state_inner)
        .transpose(2, 0, 1, 3)
        .reshape(kcount, state_width)
        .astype(f32)
    )
    state_bias = small_part(6).reshape(state_width).astype(f32)

    place = jnp.arange(width)
    feature_d = ring.rank_at(place // shard) * shard + place % shard
    inside = place % shard
    feature_g = (
        inside // piece * (width // tensor) + ring.rank_at(place // shard) * piece + inside % piece
    )
    to_d = (jnp.arange(width)[:, None] == feature_d[None, :]).astype(bf16)
    g_to_d = (feature_g[:, None] == feature_d[None, :]).astype(bf16)
    w_state = dot_tn(g_to_d, wst_g).astype(bf16)
    w_kv = dot_tn(g_to_d, wkv_g).astype(bf16)
    own_resid = dot(block_input, to_d)
    own_grad_half = dot(out_grad, to_d).astype(bf16)
    ffn_gain_f = dot(jnp.broadcast_to(ffn_gain_nat[None], (16, width)), to_d)[0]
    in_gain_d = dot(jnp.broadcast_to(small_part(3).reshape(1, width), (16, width)), to_d)[0]
    grad_all = z_gather_async(own_grad_half)

    resid_nat = rows_nat.astype(f32)
    in_scale = lax.rsqrt(jnp.mean(resid_nat * resid_nat, axis=1, keepdims=True) + norm_eps)
    normed_nat = (resid_nat * in_scale * in_gain_f[None, :]).astype(bf16)
    normed = dot(normed_nat, to_d).astype(bf16)
    normed_g = dot_nt(normed, g_to_d).astype(bf16)
    zq_lin = dot(normed, wzq)
    gate_z = zq_lin[:, :channels]
    query_lin = zq_lin[:, channels:].reshape(rows, q_local, AHD)
    xs_lin = dot(normed, wxs)
    x_lin = xs_lin[:, :channels]
    step_raw = xs_lin[:, channels : channels + heads]
    state_lin = dot(normed, w_state)
    kv_lin = dot(normed, w_kv)
    key_lin, value_lin = kv_lin[:, :AHD], kv_lin[:, AHD:]

    allowed = [None] + [(positions >= tap).astype(f32)[:, None] for tap in range(1, kcount)]
    x_pre = causal_conv(x_lin, x_taps, x_bias, allowed)
    x_act = jax.nn.silu(x_pre)
    state_pre = causal_conv(state_lin, state_taps, state_bias, allowed)
    state_act = jax.nn.silu(state_pre)
    b_matrix = state_act[:, :NSTATE].astype(bf16)
    c_matrix = state_act[:, NSTATE:].astype(bf16)
    step_size = jax.nn.softplus(step_raw + step_bias[None, :])
    decay_rate = -jnp.exp(decay_log)
    row_at = jnp.arange(rows)[:, None]
    col_at = jnp.arange(rows)[None, :]
    lower = (col_at <= row_at).astype(f32)
    cum_decay = jnp.dot(lower, step_size * decay_rate[None, :], precision=HIGHEST)
    cum_heads = cum_decay.T
    seg_mask = (col_at <= row_at) & (col_at >= row_at - positions[:, None])
    decay_mat = jnp.exp(
        jnp.where(seg_mask[None], cum_heads[:, :, None] - cum_heads[:, None, :], -jnp.inf)
    )
    gram_mat = dot_nt(c_matrix, b_matrix)
    mix_mat = (decay_mat * gram_mat[None]).astype(bf16)
    x_heads = x_act.reshape(rows, heads, HD)
    drive_in = (step_size[:, :, None] * x_heads).astype(bf16)
    ssm_out = (
        jnp.einsum("hts,shp->thp", mix_mat, drive_in, preferred_element_type=f32)
        + skip_gain[None, :, None] * x_heads
    )
    ssm_flat = ssm_out.reshape(rows, channels)
    gate_silu = jax.nn.silu(gate_z)
    gated_out = ssm_flat * gate_silu
    square_sums = z_sum(jnp.sum(gated_out * gated_out, axis=1))

    freq_rates = rope_base ** (-2.0 * jnp.arange(AHD // 2, dtype=f32) / AHD)
    angles = positions.astype(f32)[:, None] * freq_rates[None, :]
    cosine, sine = jnp.cos(angles), jnp.sin(angles)
    query_rot = rotate(query_lin, cosine[:, None, :], sine[:, None, :], 1.0).astype(bf16)
    key_rot = rotate(key_lin, cosine, sine, 1.0).astype(bf16)
    value_half = value_lin.astype(bf16)
    score_scale = AHD ** (-0.5)
    scores = (
        jnp.einsum("thd,sd->hts", query_rot, key_rot, preferred_element_type=f32) * score_scale
    )
    exp_scores = jnp.exp(jnp.where(seg_mask[None], scores, -jnp.inf))
    row_totals = jnp.sum(exp_scores, axis=2, keepdims=True)
    attn_prob_f = exp_scores / row_totals
    attn_prob = attn_prob_f.astype(bf16)
    context = (
        jnp.einsum("hts,sd->thd", attn_prob, value_half, preferred_element_type=f32)
        .astype(bf16)
        .reshape(rows, q_local * AHD)
    )
    ssm_scale = lax.rsqrt(square_sums / all_channels + norm_eps)[:, None]
    ssm_normed = (gated_out * ssm_scale * mixer_gain_f[None, :]).astype(bf16)

    mixed = z_scatter((dot_nt(ssm_normed, w_mix) + dot_nt(context, w_attn)).astype(bf16))
    hidden = own_resid + mixed
    ff_scale = lax.rsqrt(jnp.mean(hidden * hidden, axis=1, keepdims=True) + norm_eps)
    ffn_in = z_gather((hidden * ff_scale * ffn_gain_f[None, :]).astype(bf16))

    gate_lin = dot(ffn_in, w_gate)
    up_lin = dot(ffn_in, w_up)
    gate_act = jax.nn.silu(gate_lin)
    ffn_act = (gate_act * up_lin).astype(bf16)
    act_grad = dot(grad_all, w_down)
    gate_back = (act_grad * up_lin * silu_grad(gate_lin)).astype(bf16)
    up_back = (act_grad * gate_act).astype(bf16)
    ffn_back = z_scatter((dot_nt(gate_back, w_gate) + dot_nt(up_back, w_up)).astype(bf16))
    ffn_gain_part = jnp.sum(ffn_back * hidden * ff_scale, axis=0)
    ffn_norm_back = ffn_back * ffn_gain_f[None, :]
    resid_grad = (
        own_grad_half.astype(f32)
        + ff_scale * ffn_norm_back
        - hidden * ff_scale**3 * jnp.mean(ffn_norm_back * hidden, axis=1, keepdims=True)
    )
    resid_all = z_gather(resid_grad.astype(bf16))
    gate_red = ring.reduce(dot_tn(ffn_in, gate_back).astype(bf16), 0)
    up_red = ring.reduce(dot_tn(ffn_in, up_back).astype(bf16), 1)
    down_red = ring.reduce(dot_tn(grad_all, ffn_act).astype(bf16), 1).T
    ffn_rows = z_scatter(
        lax.optimization_barrier((dot_nt(ffn_act, w_down).astype(bf16), resid_all))[0]
    )
    output = dot_nt((hidden + ffn_rows).astype(bf16), to_d).astype(bf16)

    mixer_red = ring.reduce(dot_tn(resid_all, ssm_normed).astype(bf16), 0).T
    attn_red = ring.reduce(dot_tn(resid_all, context).astype(bf16), 0).T
    ssm_back = dot(resid_all, w_mix)
    ctx_back = dot(resid_all, w_attn).astype(bf16).reshape(rows, q_local, AHD)

    gain_back = ssm_back * mixer_gain_f[None, :]
    row_dots = z_sum(jnp.sum(gain_back * gated_out, axis=1))

    prob_half = attn_prob
    value_grad = jnp.einsum("hts,thd->sd", prob_half, ctx_back, preferred_element_type=f32)
    prob_grad = jnp.einsum("thd,sd->hts", ctx_back, value_half, preferred_element_type=f32)
    row_delta = jnp.sum(attn_prob_f * prob_grad, axis=2, keepdims=True)
    score_back = (attn_prob_f * (prob_grad - row_delta) * score_scale).astype(bf16)
    query_back = jnp.einsum("hts,sd->thd", score_back, key_rot, preferred_element_type=f32)
    key_back = jnp.einsum("hts,thd->sd", score_back, query_rot, preferred_element_type=f32)
    query_grad = (
        rotate(query_back, cosine[:, None, :], sine[:, None, :], -1.0)
        .astype(bf16)
        .reshape(rows, q_local * AHD)
    )
    kv_grad = jnp.concatenate([rotate(key_back, cosine, sine, -1.0), value_grad], axis=1)
    kv_grad = kv_grad.astype(bf16)
    query_red = ring.reduce(dot_tn(normed, query_grad).astype(bf16), 0)
    kv_red = ring.reduce(dot_tn(normed_g, kv_grad).astype(bf16), 0)

    mixer_gain_grad = jnp.sum(ssm_back * gated_out * ssm_scale, axis=0)
    gated_back = (
        ssm_scale * gain_back - gated_out * ssm_scale**3 * row_dots[:, None] / all_channels
    )
    out_back_flat = gated_back * gate_silu
    out_back = out_back_flat.reshape(rows, heads, HD)
    z_back = (gated_back * ssm_flat * silu_grad(gate_z)).astype(bf16)
    z_red = ring.reduce(dot_tn(normed, z_back).astype(bf16), 0)
    skip_grad = jnp.sum(out_back * x_heads, axis=(0, 2))
    out_half = out_back.astype(bf16)
    drive_back = jnp.einsum("hts,thp->shp", mix_mat, out_half, preferred_element_type=f32)
    mix_back = jnp.einsum("thp,shp->hts", out_half, drive_in, preferred_element_type=f32)
    decay_mix = mix_back * decay_mat
    gram_back = jnp.sum(decay_mix, axis=0).astype(bf16)
    pair_term = decay_mix * gram_mat[None]
    cum_back = (jnp.sum(pair_term, axis=2) - jnp.sum(pair_term, axis=1)).T
    log_decay_back = lax.dot_general(
        lower, cum_back, (((0,), (0,)), ((), ())), precision=HIGHEST, preferred_element_type=f32
    )
    c_back = dot(gram_back, b_matrix)
    b_back = dot_tn(gram_back, c_matrix)
    x_act_back = skip_gain[None, :, None] * out_back + step_size[:, :, None] * drive_back
    step_raw_back = (
        jnp.sum(drive_back * x_heads, axis=2) + log_decay_back * decay_rate[None, :]
    ) * jax.nn.sigmoid(step_raw + step_bias[None, :])
    step_bias_grad = jnp.sum(step_raw_back, axis=0)
    decay_log_grad = jnp.sum(log_decay_back * step_size, axis=0) * decay_rate
    x_pre_back = x_act_back.reshape(rows, channels) * silu_grad(x_pre)
    x_taps_grad, x_bias_grad, x_lin_back = conv_backward(x_pre_back, x_lin, x_taps, allowed)
    state_pre_back = jnp.concatenate([b_back, c_back], axis=1) * silu_grad(state_pre)
    state_taps_grad, state_bias_grad, state_lin_back = conv_backward(
        state_pre_back, state_lin, state_taps, allowed
    )
    xs_half = jnp.concatenate(
        [x_lin_back, jnp.pad(step_raw_back, ((0, 0), (0, step_pad)))], axis=1
    ).astype(bf16)
    state_half = state_lin_back.astype(bf16)
    zq_half = jnp.concatenate([z_back, query_grad], axis=1)
    normed_back = (
        dot_nt(zq_half, wzq)
        + dot_nt(xs_half, wxs)
        + dot_nt(state_half, w_state)
        + dot_nt(kv_grad, w_kv)
    )
    normed_back_own = z_scatter(normed_back.astype(bf16))
    xs_red = ring.reduce(dot_tn(normed, xs_half).astype(bf16), 1)
    state_red = ring.reduce(dot_tn(normed_g, state_half).astype(bf16), 1)

    own_in_scale = lax.rsqrt(jnp.mean(own_resid * own_resid, axis=1, keepdims=True) + norm_eps)
    in_gain_sum = jnp.sum(
        normed_back * (dot(rows_nat, to_d) * in_scale), axis=0
    )
    gains = jnp.stack([in_gain_sum, ffn_gain_part])
    gains = lax.dot_general(
        gains, to_d.astype(f32), (((1,), (1,)), ((), ())), precision=HIGHEST
    )
    inner = HD // n

    def by_rank(value):
        lead = value.size // HD
        return value.reshape(lead, n, inner).transpose(1, 0, 2).reshape(n, lead * inner)

    head_terms = jnp.concatenate([decay_log_grad, step_bias_grad, skip_grad])
    state_small = jnp.concatenate([state_taps_grad, state_bias_grad[None]], axis=0)
    per_rank = [
        by_rank(x_taps_grad),
        by_rank(x_bias_grad),
        by_rank(mixer_gain_grad),
        jnp.broadcast_to(head_terms[None], (n, 3 * heads)),
    ]
    per_both = jnp.concatenate(
        [
            gains.reshape(2, tensor, n, piece).transpose(2, 1, 0, 3).reshape(n, tensor, -1),
            state_small.reshape(kcount + 1, tensor, n, state_inner)
            .transpose(2, 1, 0, 3)
            .reshape(n, tensor, -1),
        ],
        axis=2,
    )
    both_size = per_both.shape[2]
    flat = jnp.concatenate(per_rank + [per_both.reshape(n, -1)], axis=1)
    ranks = jnp.arange(n)
    pick = (ring.rank_at(ranks)[:, None] == ranks[None, :]).astype(f32)
    flat = jnp.dot(pick, flat, precision=HIGHEST)
    flat_red = ring.reduce(flat, 0)[0]
    parts = []
    at = 0
    for item in per_rank:
        parts.append(flat_red[at : at + item.shape[1]])
        at += item.shape[1]
    x_taps_red = parts[0].reshape(kcount, heads, inner)
    x_bias_red = parts[1].reshape(heads, inner)
    mixer_gain_red = parts[2].reshape(heads, inner)
    heads_red = parts[3].reshape(3, heads)
    both_red = z_scatter(flat_red[at:].reshape(tensor, both_size))[0]
    in_gain_red = both_red[:piece]
    ffn_gain_red = both_red[piece : 2 * piece]
    state_small_red = both_red[2 * piece :].reshape(kcount + 1, state_inner)

    state_own = z_scatter(state_red.astype(bf16))
    kv_blocks = kv_red.astype(bf16).reshape(tensor, piece, 2 * AHD)
    key_cols = [jnp.zeros((piece, AHD), f32) for _ in range(KVH)]
    value_cols = [jnp.zeros((piece, AHD), f32) for _ in range(KVH)]
    for step in range(tensor):
        sent = lax.dynamic_index_in_dim(kv_blocks, (rank + step) % tensor, 0, keepdims=False)
        got = (turn(sent, step) if step else sent).astype(f32)
        head_of = (rank - step) % tensor * q_local // group_size
        for head in range(KVH):
            term = jnp.where(head_of == head, got, 0.0)
            key_cols[head] = key_cols[head] + term[:, :AHD]
            value_cols[head] = value_cols[head] + term[:, AHD:]
    keyval_red = jnp.concatenate(key_cols + value_cols, axis=1)

    in_back = normed_back_own * in_gain_d[None, :]
    input_grad = (
        resid_grad
        + own_in_scale * in_back
        - own_resid * own_in_scale**3 * jnp.mean(in_back * own_resid, axis=1, keepdims=True)
    )
    input_grad = lax.dot_general(
        input_grad, to_d.astype(f32), (((1,), (1,)), ((), ())), precision=HIGHEST
    )
    return (
        output,
        input_grad,
        in_gain_red,
        z_red,
        xs_red[:, :channels],
        xs_red[:, channels : channels + heads],
        state_own,
        x_taps_red,
        x_bias_red,
        state_small_red[:kcount],
        state_small_red[kcount],
        heads_red[0],
        heads_red[1],
        heads_red[2],
        mixer_gain_red,
        mixer_red,
        query_red,
        keyval_red,
        attn_red,
        ffn_gain_red,
        gate_red,
        up_red,
        down_red,
    )


def solution(mesh):
    in_specs = (
        P(("dp", "tensor"), None),
        P("dp"),
        P(("dp", "tensor"), None),
        P(("tensor", "dp")),
        P("dp", "tensor"),
        P("dp", "tensor"),
        P("dp", "tensor"),
        P(("tensor", "dp"), None),
        P(None, "tensor", "dp"),
        P("tensor", "dp"),
        P(None, ("tensor", "dp")),
        P(("tensor", "dp")),
        P("tensor"),
        P("tensor"),
        P("tensor"),
        P("tensor", "dp"),
        P("tensor", "dp"),
        P("dp", "tensor"),
        P(("tensor", "dp"), None),
        P("tensor", "dp"),
        P(("tensor", "dp")),
        P("dp", "tensor"),
        P("dp", "tensor"),
        P("tensor", "dp"),
    )
    out_specs = (
        P(("dp", "tensor"), None),
        P(("dp", "tensor"), None),
        P(("tensor", "dp")),
        P("dp", "tensor"),
        P("dp", "tensor"),
        P("dp", "tensor"),
        P(("tensor", "dp"), None),
        P(None, "tensor", "dp"),
        P("tensor", "dp"),
        P(None, ("tensor", "dp")),
        P(("tensor", "dp")),
        P("tensor"),
        P("tensor"),
        P("tensor"),
        P("tensor", "dp"),
        P("tensor", "dp"),
        P("dp", "tensor"),
        P(("tensor", "dp"), None),
        P("tensor", "dp"),
        P(("tensor", "dp")),
        P("dp", "tensor"),
        P("dp", "tensor"),
        P("tensor", "dp"),
    )
    return jax.shard_map(local, mesh=mesh, in_specs=in_specs, out_specs=out_specs, check_vma=False)
```

```python
import jax
import jax.numpy as jnp
from jax import lax
from jax.experimental import pallas as pl
from jax.experimental.pallas import tpu as pltpu
from jax.sharding import PartitionSpec as P

HD = 64
NSTATE = 128
KVH = 2
AHD = 128

norm_eps = 1e-05
rope_base = 10000.0
bf16 = jnp.bfloat16
f32 = jnp.float32
HIGHEST = lax.Precision.HIGHEST


def dot(left, right):
    return jnp.dot(left, right, preferred_element_type=f32)


def dot_nt(left, right):
    return lax.dot_general(left, right, (((1,), (1,)), ((), ())), preferred_element_type=f32)


def dot_tn(left, right):
    return lax.dot_general(left, right, (((0,), (0,)), ((), ())), preferred_element_type=f32)


def sigmoid(values):
    return 1.0 / (1.0 + jnp.exp(-values))


def silu_grad(values):
    part = sigmoid(values)
    return part * (1.0 + values * (1.0 - part))


def exact(left, right, dims):
    return lax.dot_general(
        left, right, (dims, ((), ())), precision=HIGHEST, preferred_element_type=f32
    )


def iota(shape, axis):
    return lax.broadcasted_iota(jnp.int32, shape, axis)


def segment_mask(position):
    rows = position.shape[0]
    row_at, col_at = iota((rows, rows), 0), iota((rows, rows), 1)
    return (col_at <= row_at) & (col_at >= row_at - position)


def conv(values, taps, bias, position):
    total = bias + taps[0:1, :] * values
    for tap in range(1, taps.shape[0]):
        moved = jnp.where(position >= tap, pltpu.roll(values, tap, 0), 0.0)
        total = total + taps[tap : tap + 1, :] * moved
    return total


def conv_back(grad, values, taps, position):
    rows = grad.shape[0]
    tap_grads = [jnp.sum(grad * values, axis=0, keepdims=True)]
    total = taps[0:1, :] * grad
    for tap in range(1, taps.shape[0]):
        masked = jnp.where(position >= tap, grad, 0.0)
        moved = pltpu.roll(values, tap, 0)
        tap_grads.append(jnp.sum(masked * moved, axis=0, keepdims=True))
        total = total + taps[tap : tap + 1, :] * pltpu.roll(masked, rows - tap, 0)
    return tap_grads, jnp.sum(grad, axis=0, keepdims=True), total


def decay_of(mask, cum, cum_t, head):
    apart = cum[:, head : head + 1] - cum_t[head : head + 1, :]
    return jnp.exp(jnp.where(mask, apart, -1e30))


def per_lane(values, pair):
    rows = values.shape[0]
    low = iota((rows, 2 * HD), 1) < HD
    return jnp.where(
        low, values[:, 2 * pair : 2 * pair + 1], values[:, 2 * pair + 1 : 2 * pair + 2]
    )


def ssm_forward_kernel(
    zq_ref, xs_ref, sk_ref, pos_ref, taps_ref, bias_ref, staps_ref, sbias_ref, head_ref, skip_ref,
    gated_ref, flat_ref, xpre_ref, spre_ref, drive_ref, step_ref, cum_ref, cumt_ref,
):
    rows = zq_ref.shape[0]
    channels = gated_ref.shape[1]
    states = spre_ref.shape[1]
    position = pos_ref[...]
    x_pre = conv(xs_ref[:, :channels], taps_ref[...], bias_ref[...], position)
    xpre_ref[...] = x_pre
    x_act = x_pre * sigmoid(x_pre)
    state_pre = conv(sk_ref[:, :states], staps_ref[...], sbias_ref[...], position)
    spre_ref[...] = state_pre
    state_act = (state_pre * sigmoid(state_pre)).astype(bf16)
    b_matrix, c_matrix = state_act[:, : states // 2], state_act[:, states // 2 :]
    raw = xs_ref[:, channels:] + head_ref[0:1, :]
    step = jnp.maximum(raw, 0.0) + jnp.log1p(jnp.exp(-jnp.abs(raw)))
    step_ref[...] = step
    paced = step * head_ref[1:2, :]
    row_at, col_at = iota((rows, rows), 0), iota((rows, rows), 1)
    lower = (col_at <= row_at).astype(f32)
    upper = (row_at <= col_at).astype(f32)
    cum = exact(lower, paced, ((1,), (0,)))
    cum_t = exact(paced, upper, ((0,), (0,)))
    cum_ref[...] = cum
    cumt_ref[...] = cum_t
    mask = segment_mask(position)
    gram = dot_nt(c_matrix, b_matrix)
    low = iota((rows, 2 * HD), 1) < HD
    for pair in range(channels // (2 * HD)):
        lanes = slice(2 * HD * pair, 2 * HD * (pair + 1))
        act = x_act[:, lanes]
        drive = (per_lane(step, pair) * act).astype(bf16)
        drive_ref[:, lanes] = drive
        outs = []
        for side in range(2):
            mix = (decay_of(mask, cum, cum_t, 2 * pair + side) * gram).astype(bf16)
            outs.append(dot(mix, drive))
        out = jnp.where(low, outs[0], outs[1]) + skip_ref[0:1, lanes] * act
        flat_ref[:, lanes] = out
        gate = zq_ref[:, lanes]
        gated_ref[:, lanes] = out * (gate * sigmoid(gate))


def attention_forward_kernel(
    zq_ref, sk_ref, pos_ref, cos_ref, sin_ref, ctx_ref, prob_ref, q_ref, k_ref, v_ref
):
    heads = prob_ref.shape[0]
    first = zq_ref.shape[1] - heads * AHD
    last = sk_ref.shape[1]
    cosine, sine = cos_ref[...], sin_ref[...]
    mask = segment_mask(pos_ref[...])
    key = sk_ref[:, last - 2 * AHD : last - AHD]
    key = (key * cosine + pltpu.roll(key, AHD // 2, 1) * sine).astype(bf16)
    value = sk_ref[:, last - AHD :].astype(bf16)
    k_ref[...] = key
    v_ref[...] = value
    for head in range(heads):
        lanes = slice(AHD * head, AHD * (head + 1))
        query = zq_ref[:, first + AHD * head : first + AHD * (head + 1)]
        query = (query * cosine + pltpu.roll(query, AHD // 2, 1) * sine).astype(bf16)
        q_ref[:, lanes] = query
        scores = dot_nt(query, key) * AHD ** (-0.5)
        weights = jnp.where(mask, jnp.exp(jnp.where(mask, scores, 0.0)), 0.0)
        prob = weights / jnp.sum(weights, axis=1, keepdims=True)
        prob_ref[head] = prob
        ctx_ref[:, lanes] = dot(prob.astype(bf16), value).astype(bf16)


def attention_backward_kernel(
    prob_ref, q_ref, k_ref, v_ref, back_ref, cos_ref, sin_ref, qgrad_ref, kvgrad_ref
):
    heads = prob_ref.shape[0]
    cosine, sine = cos_ref[...], sin_ref[...]
    key, value = k_ref[...], v_ref[...]

    def unrotate(grad):
        return grad * cosine - pltpu.roll(grad, AHD // 2, 1) * sine

    key_total = None
    value_total = None
    for head in range(heads):
        lanes = slice(AHD * head, AHD * (head + 1))
        back = back_ref[:, lanes].astype(bf16)
        prob = prob_ref[head]
        value_part = dot_tn(prob.astype(bf16), back)
        prob_grad = dot_nt(back, value)
        delta = jnp.sum(prob * prob_grad, axis=1, keepdims=True)
        score_back = (prob * (prob_grad - delta) * AHD ** (-0.5)).astype(bf16)
        qgrad_ref[:, lanes] = unrotate(dot(score_back, key)).astype(bf16)
        key_part = dot_tn(score_back, q_ref[:, lanes])
        key_total = key_part if head == 0 else key_total + key_part
        value_total = value_part if head == 0 else value_total + value_part
    kvgrad_ref[:, :AHD] = unrotate(key_total).astype(bf16)
    kvgrad_ref[:, AHD:] = value_total.astype(bf16)


def ssm_backward_kernel(
    sback_ref, gated_ref, scale_ref, gain_ref, zq_ref, flat_ref, xpre_ref, xs_ref, sk_ref,
    spre_ref, drive_ref, step_ref, cum_ref, cumt_ref, pos_ref, taps_ref, staps_ref, head_ref,
    skip_ref, zback_ref, xback_ref, stback_ref, wide_ref, state_ref, lane_ref,
):
    rows, channels = gated_ref.shape
    states = spre_ref.shape[1]
    kcount = taps_ref.shape[0]
    position = pos_ref[...]
    mask = segment_mask(position)
    state_pre = spre_ref[...]
    state_act = (state_pre * sigmoid(state_pre)).astype(bf16)
    b_matrix, c_matrix = state_act[:, : states // 2], state_act[:, states // 2 :]
    gram = dot_nt(c_matrix, b_matrix)
    step, cum, cum_t = step_ref[...], cum_ref[...], cumt_ref[...]
    scale, pull = scale_ref[:, 0:1], scale_ref[:, 1:2]
    width = step.shape[1]
    low = iota((rows, 2 * HD), 1) < HD
    lane = iota((rows, width), 1)
    line = iota((width, rows), 0)
    gram_back = jnp.zeros((rows, rows), f32)
    row_sums = jnp.zeros((rows, width), f32)
    col_sums = jnp.zeros((width, rows), f32)
    raw_back = jnp.zeros((rows, width), f32)
    wide_ref[...] = jnp.zeros_like(wide_ref)
    state_ref[...] = jnp.zeros_like(state_ref)
    lane_ref[...] = jnp.zeros_like(lane_ref)
    for pair in range(channels // (2 * HD)):
        lanes = slice(2 * HD * pair, 2 * HD * (pair + 1))
        back, gated = sback_ref[:, lanes], gated_ref[:, lanes]
        wide_ref[kcount + 1 : kcount + 2, lanes] = jnp.sum(
            back * gated * scale, axis=0, keepdims=True
        )
        gated_back = scale * (back * gain_ref[0:1, lanes]) - gated * pull
        gate = zq_ref[:, lanes]
        part = sigmoid(gate)
        out_back = gated_back * (gate * part)
        zback_ref[:, lanes] = (
            gated_back * flat_ref[:, lanes] * (part * (1.0 + gate * (1.0 - part)))
        ).astype(bf16)
        x_pre = xpre_ref[:, lanes]
        x_part = sigmoid(x_pre)
        act = x_pre * x_part
        wide_ref[kcount + 2 : kcount + 3, lanes] = jnp.sum(out_back * act, axis=0, keepdims=True)
        out_half = out_back.astype(bf16)
        drive = drive_ref[:, lanes]
        backs = []
        for side in range(2):
            head = 2 * pair + side
            decay = decay_of(mask, cum, cum_t, head)
            mix = decay * gram
            backs.append(dot_tn(mix.astype(bf16), out_half))
            inside = low if side == 0 else jnp.logical_not(low)
            mine = jnp.where(inside, out_back, 0.0).astype(bf16)
            mix_back = dot_nt(mine, drive)
            gram_back = gram_back + mix_back * decay
            pairs = mix_back * mix
            row_sums = jnp.where(lane == head, jnp.sum(pairs, axis=1, keepdims=True), row_sums)
            col_sums = jnp.where(line == head, jnp.sum(pairs, axis=0, keepdims=True), col_sums)
        drive_back = jnp.where(low, backs[0], backs[1])
        product = drive_back * act
        for side in range(2):
            inside = low if side == 0 else jnp.logical_not(low)
            summed = jnp.sum(jnp.where(inside, product, 0.0), axis=1, keepdims=True)
            raw_back = jnp.where(lane == 2 * pair + side, summed, raw_back)
        act_back = skip_ref[0:1, lanes] * out_back + per_lane(step, pair) * drive_back
        pre_back = act_back * (x_part * (1.0 + x_pre * (1.0 - x_part)))
        tap_grads, bias_grad, x_back = conv_back(
            pre_back, xs_ref[:, lanes], taps_ref[:, lanes], position
        )
        for tap in range(kcount):
            wide_ref[tap : tap + 1, lanes] = tap_grads[tap]
        wide_ref[kcount : kcount + 1, lanes] = bias_grad
        xback_ref[:, lanes] = x_back.astype(bf16)
    row_at, col_at = iota((rows, rows), 0), iota((rows, rows), 1)
    upper = (row_at <= col_at).astype(f32)
    log_back = exact(upper, row_sums, ((1,), (0,))) - exact(upper, col_sums, ((1,), (1,)))
    rate = head_ref[1:2, :]
    raw_back = (raw_back + log_back * rate) * sigmoid(xs_ref[:, channels:] + head_ref[0:1, :])
    xback_ref[:, channels:] = raw_back.astype(bf16)
    lane_ref[0:1, :] = jnp.sum(raw_back, axis=0, keepdims=True)
    lane_ref[1:2, :] = jnp.sum(log_back * step, axis=0, keepdims=True) * rate
    gram_half = gram_back.astype(bf16)
    state_part = sigmoid(state_pre)
    state_slope = state_part * (1.0 + state_pre * (1.0 - state_part))
    sides = (dot_tn(gram_half, c_matrix), dot(gram_half, b_matrix))
    for side in range(2):
        cols = slice(states // 2 * side, states // 2 * (side + 1))
        tap_grads, bias_grad, s_back = conv_back(
            sides[side] * state_slope[:, cols], sk_ref[:, cols], staps_ref[:, cols], position
        )
        for tap in range(kcount):
            state_ref[tap : tap + 1, cols] = tap_grads[tap]
        state_ref[kcount : kcount + 1, cols] = bias_grad
        stback_ref[:, cols] = s_back.astype(bf16)


def call(kernel, outs, flops, *args):
    moved = sum(item.size * item.dtype.itemsize for item in args)
    moved += sum(item.size * item.dtype.itemsize for item in outs)
    return pl.pallas_call(
        kernel,
        out_shape=outs,
        cost_estimate=pl.CostEstimate(flops=flops, bytes_accessed=moved, transcendentals=0),
        compiler_params=pltpu.CompilerParams(vmem_limit_bytes=40 << 20),
    )(*args)


def shape(dtype, *dims):
    return jax.ShapeDtypeStruct(dims, dtype)


class Ring:
    def __init__(self):
        self.count = lax.axis_size("dp")
        self.me = lax.axis_index("dp")
        bits = []
        bit = 2
        while bit < self.count:
            bits.append(bit)
            bit *= 2
        self.high_first = bits[::-1]
        self.orders = (bits, bits[::-1])

    def swap(self, value, bit):
        return lax.ppermute(value, "dp", [(i, i ^ bit) for i in range(self.count)])

    def rank_at(self, place):
        half = self.count // 2
        return self.me ^ ((place % half) * 2 + place // half)

    def gather(self, shard, kind):
        have = []
        value = shard
        lead = 0
        first = None
        for bit in self.orders[kind]:
            axis = sum(1 for other in have if other > bit)
            got = self.swap(value, bit)
            first = got if first is None else first
            value = jnp.stack([value, got], axis=axis)
            have.append(bit)
            lead += 1
        flat = (self.count // 2 * shard.shape[0],) + shard.shape[1:]
        return (value.reshape(flat), self.swap(value, 1).reshape(flat)), first

    def reduce(self, value, kind):
        wire = value.dtype
        levels = len(self.high_first)
        rest = (value.shape[0] // self.count,) + value.shape[1:]
        value = value.reshape((2,) * (levels + 1) + rest)
        total = value[0].astype(f32) + self.swap(value[1], 1).astype(f32)
        left = list(self.high_first)
        for bit in self.orders[1 - kind]:
            axis = left.index(bit)
            keep = lax.index_in_dim(total, 0, axis, keepdims=False)
            send = lax.index_in_dim(total, 1, axis, keepdims=False).astype(wire)
            total = keep + self.swap(send, bit).astype(f32)
            left.remove(bit)
        return total


def turn(value, step):
    count = lax.axis_size("tensor")
    return lax.ppermute(value, "tensor", [(i, (i + step) % count) for i in range(count)])


def z_sum(value):
    total = value
    for step in range(1, lax.axis_size("tensor")):
        total = total + turn(value, step)
    return total


def z_scatter(value):
    count = lax.axis_size("tensor")
    rank = lax.axis_index("tensor")
    blocks = value.reshape((count, value.shape[0] // count) + value.shape[1:])

    def block(step):
        return lax.dynamic_index_in_dim(blocks, (rank + step) % count, 0, keepdims=False)

    got = [turn(block(step), step) for step in range(1, count)]
    total = block(0).astype(f32)
    for part in got:
        total = total + part.astype(f32)
    return total


def z_gather_async(value):
    count = lax.axis_size("tensor")
    rank = lax.axis_index("tensor")
    whole = jnp.zeros((count,) + value.shape, value.dtype)
    whole = lax.dynamic_update_index_in_dim(whole, value, rank, 0)
    for step in range(1, count):
        whole = lax.dynamic_update_index_in_dim(
            whole, turn(value, step), (rank - step) % count, 0
        )
    return whole.reshape((count * value.shape[0],) + value.shape[1:])


def z_gather(value):
    return lax.all_gather(value, "tensor", axis=0, tiled=True)


def local(
    block_input,
    positions,
    out_grad,
    in_gain,
    z_proj,
    x_proj,
    step_proj,
    state_proj,
    x_conv,
    x_conv_bias,
    state_conv,
    state_conv_bias,
    decay_log,
    step_bias,
    skip_gain,
    mixer_gain,
    mixer_out,
    query_proj,
    keyval_proj,
    attn_out,
    ffn_gain,
    gate_proj,
    up_proj,
    down_proj,
):
    ring = Ring()
    n = ring.count
    tensor = lax.axis_size("tensor")
    rank = lax.axis_index("tensor")
    width = block_input.shape[1]
    own_rows = block_input.shape[0]
    rows = own_rows * tensor
    heads = decay_log.shape[0]
    channels = heads * HD
    all_channels = channels * tensor
    shard = width // n
    piece = width // (n * tensor)
    kcount = x_conv.shape[0]
    q_local = query_proj.shape[1] // AHD
    group_size = q_local * tensor // KVH
    kv_head = rank * q_local // group_size
    state_width = 2 * NSTATE

    step_pad = (-heads) % 128
    small = [x_conv, x_conv_bias, mixer_gain, in_gain, ffn_gain, state_conv, state_conv_bias]
    offsets = [0]
    for item in small:
        offsets.append(offsets[-1] + item.size)
    small_flat = jnp.concatenate([item.reshape(-1) for item in small])
    pack_width = state_width + keyval_proj.shape[1]
    small_flat = jnp.pad(small_flat, (0, (-small_flat.size) % pack_width)).reshape(-1, pack_width)
    joined = jnp.concatenate(
        [jnp.concatenate([state_proj, keyval_proj], axis=1), small_flat], axis=0
    )
    joined = z_gather_async(joined).reshape(tensor, -1, pack_width)

    wzq, first_a = ring.gather(jnp.concatenate([z_proj, query_proj], axis=1), 0)
    wxs, first_b = ring.gather(
        jnp.concatenate([x_proj, jnp.pad(step_proj, ((0, 0), (0, step_pad)))], axis=1), 1
    )
    rows_nat = z_gather_async(block_input)
    shared = joined[:, :piece].reshape(shard, pack_width)
    small_rows = joined[:, piece:].reshape(shard, -1)
    small_cols = small_rows.shape[1]
    wide = jnp.concatenate(
        [
            shared[:, :state_width],
            lax.dynamic_slice_in_dim(shared, state_width + kv_head * AHD, AHD, 1),
            lax.dynamic_slice_in_dim(shared, state_width + KVH * AHD + kv_head * AHD, AHD, 1),
            jnp.pad(small_rows, ((0, 0), (0, (-small_cols) % 128))),
        ],
        axis=1,
    )
    wide_parts, _ = ring.gather(wide, 0)

    late = jnp.concatenate([mixer_out.T, attn_out.T, gate_proj, up_proj, down_proj.T], axis=1)
    late, _, _ = lax.optimization_barrier((late, first_a, first_b))
    late_all = lax.all_gather(late, "dp", axis=0, tiled=True)
    cuts = [0]
    for item in (mixer_out.shape[0], attn_out.shape[0], gate_proj.shape[1], up_proj.shape[1], down_proj.shape[0]):
        cuts.append(cuts[-1] + item)
    w_mix, w_attn, w_gate, w_up, w_down = (
        late_all[:, cuts[i] : cuts[i + 1]] for i in range(5)
    )
    w_gu = late_all[:, cuts[2] : cuts[4]]
    ffl = gate_proj.shape[1]

    small_at = state_width + 2 * AHD
    ranks = jnp.arange(n)
    pick = (ring.rank_at(ranks)[:, None] == ranks[None, :]).astype(f32)
    smalls = jnp.concatenate(
        [part[:, small_at : small_at + small_cols] for part in wide_parts], axis=0
    ).reshape(n, -1)
    smalls = dot_tn(pick.astype(bf16), smalls).astype(bf16)
    smalls = smalls.reshape(n, tensor, -1).transpose(1, 0, 2)

    def small_part(index):
        return smalls[:, :, offsets[index] : offsets[index + 1]]

    def own_small(index, lead):
        mine = lax.dynamic_index_in_dim(small_part(index), rank, 0, keepdims=False)
        return (
            mine.reshape(n, lead, HD // n).transpose(1, 0, 2).reshape(lead, HD).astype(f32)
        )

    x_taps = own_small(0, kcount * heads).reshape(kcount, channels)
    x_bias = own_small(1, heads).reshape(channels)
    mixer_gain_f = own_small(2, heads).reshape(channels)
    in_gain_f = small_part(3).reshape(width).astype(f32)
    ffn_gain_f = small_part(4).reshape(width).astype(f32)
    state_inner = state_width // (n * tensor)
    state_taps = (
        small_part(5)
        .reshape(tensor, n, kcount, state_inner)
        .transpose(2, 0, 1, 3)
        .reshape(kcount, state_width)
        .astype(f32)
    )
    state_bias = small_part(6).reshape(state_width).astype(f32)

    place = jnp.arange(width)
    feature_d = ring.rank_at(place // shard) * shard + place % shard
    inside = place % shard
    feature_g = (
        inside // piece * (width // tensor) + ring.rank_at(place // shard) * piece + inside % piece
    )
    to_d = (place[:, None] == feature_d[None, :]).astype(bf16)
    to_g = (place[:, None] == feature_g[None, :]).astype(bf16)
    half = width // 2
    w_sk = (
        dot(to_g[:, :half], wide_parts[0][:, :small_at])
        + dot(to_g[:, half:], wide_parts[1][:, :small_at])
    ).astype(bf16)
    own_resid = block_input.astype(f32)
    grad_all = z_gather_async(out_grad)

    resid_nat = rows_nat.astype(f32)
    in_scale = lax.rsqrt(jnp.mean(resid_nat * resid_nat, axis=1, keepdims=True) + norm_eps)
    normed_nat = (resid_nat * in_scale * in_gain_f[None, :]).astype(bf16)
    normed = dot(normed_nat, to_d).astype(bf16)
    normed_g = dot(normed_nat, to_g).astype(bf16)
    zq_lin = dot(normed[:, :half], wzq[0]) + dot(normed[:, half:], wzq[1])
    gate_z = zq_lin[:, :channels]
    query_lin = zq_lin[:, channels:].reshape(rows, q_local, AHD)
    xs_lin = dot(normed[:, :half], wxs[0]) + dot(normed[:, half:], wxs[1])
    x_lin = xs_lin[:, :channels]
    step_raw = xs_lin[:, channels : channels + heads]
    sk_lin = dot(normed_nat, w_sk)
    position = positions.reshape(rows, 1)
    decay_rate = -jnp.exp(decay_log)
    lanes_pad = (0, step_pad)
    head_rows = jnp.stack([jnp.pad(step_bias, lanes_pad), jnp.pad(decay_rate, lanes_pad)])
    skip_row = jnp.repeat(skip_gain, HD)[None]
    step_width = heads + step_pad
    gated_out, ssm_flat, x_pre, state_pre, drive_in, step_size, cum, cum_t = call(
        ssm_forward_kernel,
        (
            shape(f32, rows, channels),
            shape(f32, rows, channels),
            shape(f32, rows, channels),
            shape(f32, rows, state_width),
            shape(bf16, rows, channels),
            shape(f32, rows, step_width),
            shape(f32, rows, step_width),
            shape(f32, step_width, rows),
        ),
        2 * 10**9,
        zq_lin, xs_lin, sk_lin, position, x_taps, x_bias[None], state_taps, state_bias[None],
        head_rows, skip_row,
    )
    square_sums = z_sum(jnp.sum(gated_out * gated_out, axis=1))
    freq_rates = rope_base ** (-2.0 * jnp.arange(AHD // 2, dtype=f32) / AHD)
    angles = positions.astype(f32)[:, None] * freq_rates[None, :]
    cosine, sine = jnp.cos(angles), jnp.sin(angles)
    cosine = jnp.concatenate([cosine, cosine], axis=1)
    sine = jnp.concatenate([-sine, sine], axis=1)
    context, prob, query_rot, key_rot, value_half = call(
        attention_forward_kernel,
        (
            shape(bf16, rows, q_local * AHD),
            shape(f32, q_local, rows, rows),
            shape(bf16, rows, q_local * AHD),
            shape(bf16, rows, AHD),
            shape(bf16, rows, AHD),
        ),
        2 * 10**9,
        zq_lin, sk_lin, position, cosine, sine,
    )
    ssm_scale = lax.rsqrt(square_sums / all_channels + norm_eps)[:, None]
    ssm_normed = (gated_out * ssm_scale * mixer_gain_f[None, :]).astype(bf16)

    mixed = z_scatter((dot_nt(ssm_normed, w_mix) + dot_nt(context, w_attn)).astype(bf16))
    hidden = own_resid + mixed
    ff_scale = lax.rsqrt(jnp.mean(hidden * hidden, axis=1, keepdims=True) + norm_eps)
    ffn_in = z_gather((hidden * ff_scale * ffn_gain_f[None, :]).astype(bf16))

    gu_lin = dot(ffn_in, w_gu)
    gate_lin, up_lin = gu_lin[:, :ffl], gu_lin[:, ffl:]
    gate_act = jax.nn.silu(gate_lin)
    ffn_act = (gate_act * up_lin).astype(bf16)
    act_grad = dot(grad_all, w_down)
    gate_back = (act_grad * up_lin * silu_grad(gate_lin)).astype(bf16)
    up_back = (act_grad * gate_act).astype(bf16)
    gu_back = jnp.concatenate([gate_back, up_back], axis=1)
    ffn_back = z_scatter(dot_nt(gu_back, w_gu).astype(bf16))
    ffn_gain_part = jnp.sum(ffn_back * hidden * ff_scale, axis=0)
    ffn_norm_back = ffn_back * ffn_gain_f[None, :]
    resid_grad = (
        out_grad.astype(f32)
        + ff_scale * ffn_norm_back
        - hidden * ff_scale**3 * jnp.mean(ffn_norm_back * hidden, axis=1, keepdims=True)
    )
    resid_all = z_gather(resid_grad.astype(bf16))
    ffn_pack = jnp.concatenate(
        [dot_tn(ffn_in, gu_back).astype(bf16), dot_tn(grad_all, ffn_act).astype(bf16)], axis=1
    )
    ffn_red = lax.psum_scatter(ffn_pack, "dp", scatter_dimension=0, tiled=True).astype(f32)
    gate_red = ffn_red[:, :ffl]
    up_red = ffn_red[:, ffl : 2 * ffl]
    down_red = ffn_red[:, 2 * ffl :].T
    ffn_rows = z_scatter(
        lax.optimization_barrier((dot_nt(ffn_act, w_down).astype(bf16), resid_all))[0]
    )
    output = (hidden + ffn_rows).astype(bf16)

    ssm_back = dot(resid_all, w_mix)
    ctx_back = dot(resid_all, w_attn)
    row_dots = z_sum(jnp.sum(ssm_back * mixer_gain_f[None, :] * gated_out, axis=1))
    query_grad, kv_grad = call(
        attention_backward_kernel,
        (shape(bf16, rows, q_local * AHD), shape(bf16, rows, 2 * AHD)),
        2 * 10**9,
        prob, query_rot, key_rot, value_half, ctx_back, cosine, sine,
    )
    pull = ssm_scale**3 * row_dots[:, None] / all_channels
    z_back, xs_half, state_half, wide_sums, state_sums, lane_sums = call(
        ssm_backward_kernel,
        (
            shape(bf16, rows, channels),
            shape(bf16, rows, channels + step_width),
            shape(bf16, rows, state_width),
            shape(f32, kcount + 4, channels),
            shape(f32, kcount + 4, state_width),
            shape(f32, 8, step_width),
        ),
        4 * 10**9,
        ssm_back, gated_out, jnp.concatenate([ssm_scale, pull], axis=1), mixer_gain_f[None],
        zq_lin, ssm_flat, x_pre, xs_lin, sk_lin, state_pre, drive_in, step_size, cum, cum_t,
        position, x_taps, state_taps, head_rows, skip_row,
    )
    x_taps_grad = wide_sums[:kcount]
    x_bias_grad = wide_sums[kcount]
    mixer_gain_grad = wide_sums[kcount + 1]
    skip_grad = jnp.sum(wide_sums[kcount + 2].reshape(heads, HD), axis=1)
    step_bias_grad = lane_sums[0, :heads]
    decay_log_grad = lane_sums[1, :heads]
    zq_half = jnp.concatenate([z_back, query_grad], axis=1)
    mid_pack = jnp.concatenate(
        [
            dot_tn(resid_all, jnp.concatenate([ssm_normed, context], axis=1)).astype(bf16),
            dot_tn(normed_nat, zq_half).astype(bf16),
        ],
        axis=1,
    )
    mid_red = lax.psum_scatter(mid_pack, "dp", scatter_dimension=0, tiled=True).astype(f32)
    qwide = q_local * AHD
    mixer_red = mid_red[:, :channels].T
    attn_red = mid_red[:, channels : channels + qwide].T
    z_red = mid_red[:, channels + qwide : 2 * channels + qwide]
    query_red = mid_red[:, 2 * channels + qwide :]
    sk_half = jnp.concatenate([state_half, kv_grad], axis=1)
    part_d = [
        (dot_nt(zq_half, wzq[i]) + dot_nt(xs_half, wxs[i])).astype(bf16) for i in range(2)
    ]
    normed_back = (
        dot_nt(part_d[0], to_d[:, :half]) + dot_nt(part_d[1], to_d[:, half:])
        + dot_nt(sk_half, w_sk)
    )
    normed_back_own = z_scatter(normed_back.astype(bf16))
    xs_red = ring.reduce(dot_tn(normed, xs_half).astype(bf16), 1)
    sk_red = ring.reduce(dot_tn(normed_g, sk_half).astype(bf16), 0)

    own_in_scale = lax.rsqrt(jnp.mean(own_resid * own_resid, axis=1, keepdims=True) + norm_eps)
    in_gain_sum = jnp.sum(normed_back * resid_nat * in_scale, axis=0)
    gains = jnp.stack([in_gain_sum, ffn_gain_part])
    inner = HD // n

    def by_rank(value):
        lead = value.size // HD
        return value.reshape(lead, n, inner).transpose(1, 0, 2).reshape(n, lead * inner)

    head_terms = jnp.concatenate([decay_log_grad, step_bias_grad, skip_grad])
    state_small = state_sums[: kcount + 1]
    per_rank = [
        by_rank(x_taps_grad),
        by_rank(x_bias_grad),
        by_rank(mixer_gain_grad),
        jnp.broadcast_to(head_terms[None], (n, 3 * heads)),
    ]
    per_both = jnp.concatenate(
        [
            gains.reshape(2, tensor, n, piece).transpose(2, 1, 0, 3).reshape(n, tensor, -1),
            state_small.reshape(kcount + 1, tensor, n, state_inner)
            .transpose(2, 1, 0, 3)
            .reshape(n, tensor, -1),
        ],
        axis=2,
    )
    both_size = per_both.shape[2]
    flat = jnp.concatenate(per_rank + [per_both.reshape(n, -1)], axis=1)
    flat = jnp.dot(pick, flat, precision=HIGHEST)
    flat_red = ring.reduce(flat, 0)[0]
    parts = []
    at = 0
    for item in per_rank:
        parts.append(flat_red[at : at + item.shape[1]])
        at += item.shape[1]
    x_taps_red = parts[0].reshape(kcount, heads, inner)
    x_bias_red = parts[1].reshape(heads, inner)
    mixer_gain_red = parts[2].reshape(heads, inner)
    heads_red = parts[3].reshape(3, heads)
    both_red = z_scatter(flat_red[at:].reshape(tensor, both_size))[0]
    in_gain_red = both_red[:piece]
    ffn_gain_red = both_red[piece : 2 * piece]
    state_small_red = both_red[2 * piece :].reshape(kcount + 1, state_inner)

    sk_blocks = sk_red.astype(bf16).reshape(tensor, piece, -1)
    state_own = jnp.zeros((piece, state_width), f32)
    key_cols = [jnp.zeros((piece, AHD), f32) for _ in range(KVH)]
    value_cols = [jnp.zeros((piece, AHD), f32) for _ in range(KVH)]
    for step in range(tensor):
        sent = lax.dynamic_index_in_dim(sk_blocks, (rank + step) % tensor, 0, keepdims=False)
        got = (turn(sent, step) if step else sent).astype(f32)
        head_of = (rank - step) % tensor * q_local // group_size
        state_own = state_own + got[:, :state_width]
        for head in range(KVH):
            term = jnp.where(head_of == head, got[:, state_width:], 0.0)
            key_cols[head] = key_cols[head] + term[:, :AHD]
            value_cols[head] = value_cols[head] + term[:, AHD:]
    keyval_red = jnp.concatenate(key_cols + value_cols, axis=1)

    in_back = normed_back_own * in_gain_f[None, :]
    input_grad = (
        resid_grad
        + own_in_scale * in_back
        - own_resid * own_in_scale**3 * jnp.mean(in_back * own_resid, axis=1, keepdims=True)
    )
    return (
        output,
        input_grad,
        in_gain_red,
        z_red,
        xs_red[:, :channels],
        xs_red[:, channels : channels + heads],
        state_own,
        x_taps_red,
        x_bias_red,
        state_small_red[:kcount],
        state_small_red[kcount],
        heads_red[0],
        heads_red[1],
        heads_red[2],
        mixer_gain_red,
        mixer_red,
        query_red,
        keyval_red,
        attn_red,
        ffn_gain_red,
        gate_red,
        up_red,
        down_red,
    )


def solution(mesh):
    in_specs = (
        P(("dp", "tensor"), None),
        P("dp"),
        P(("dp", "tensor"), None),
        P(("tensor", "dp")),
        P("dp", "tensor"),
        P("dp", "tensor"),
        P("dp", "tensor"),
        P(("tensor", "dp"), None),
        P(None, "tensor", "dp"),
        P("tensor", "dp"),
        P(None, ("tensor", "dp")),
        P(("tensor", "dp")),
        P("tensor"),
        P("tensor"),
        P("tensor"),
        P("tensor", "dp"),
        P("tensor", "dp"),
        P("dp", "tensor"),
        P(("tensor", "dp"), None),
        P("tensor", "dp"),
        P(("tensor", "dp")),
        P("dp", "tensor"),
        P("dp", "tensor"),
        P("tensor", "dp"),
    )
    out_specs = (
        P(("dp", "tensor"), None),
        P(("dp", "tensor"), None),
        P(("tensor", "dp")),
        P("dp", "tensor"),
        P("dp", "tensor"),
        P("dp", "tensor"),
        P(("tensor", "dp"), None),
        P(None, "tensor", "dp"),
        P("tensor", "dp"),
        P(None, ("tensor", "dp")),
        P(("tensor", "dp")),
        P("tensor"),
        P("tensor"),
        P("tensor"),
        P("tensor", "dp"),
        P("tensor", "dp"),
        P("dp", "tensor"),
        P(("tensor", "dp"), None),
        P("tensor", "dp"),
        P(("tensor", "dp")),
        P("dp", "tensor"),
        P("dp", "tensor"),
        P("tensor", "dp"),
    )
    return jax.shard_map(local, mesh=mesh, in_specs=in_specs, out_specs=out_specs, check_vma=False)
```

```python
import functools

import jax
import jax.numpy as jnp
from jax import lax
from jax.experimental import pallas as pl
from jax.experimental.pallas import tpu as pltpu
from jax.sharding import PartitionSpec as P

HD = 64
NSTATE = 128
KVH = 2
AHD = 128

norm_eps = 1e-05
rope_base = 10000.0
bf16 = jnp.bfloat16
f32 = jnp.float32
HIGHEST = lax.Precision.HIGHEST


def dot(left, right):
    return jnp.dot(left, right, preferred_element_type=f32)


def dot_nt(left, right):
    return lax.dot_general(left, right, (((1,), (1,)), ((), ())), preferred_element_type=f32)


def dot_tn(left, right):
    return lax.dot_general(left, right, (((0,), (0,)), ((), ())), preferred_element_type=f32)


def sigmoid(values):
    return 1.0 / (1.0 + jnp.exp(-values))


def silu_grad(values):
    part = sigmoid(values)
    return part * (1.0 + values * (1.0 - part))


def exact(left, right, dims):
    return lax.dot_general(
        left, right, (dims, ((), ())), precision=HIGHEST, preferred_element_type=f32
    )


def iota(shape, axis):
    return lax.broadcasted_iota(jnp.int32, shape, axis)


def segment_mask(position):
    rows = position.shape[0]
    row_at, col_at = iota((rows, rows), 0), iota((rows, rows), 1)
    return (col_at <= row_at) & (col_at >= row_at - position)


def conv(values, taps, bias, position):
    total = bias + taps[0:1, :] * values
    for tap in range(1, taps.shape[0]):
        moved = jnp.where(position >= tap, pltpu.roll(values, tap, 0), 0.0)
        total = total + taps[tap : tap + 1, :] * moved
    return total


def conv_back(grad, values, taps, position):
    rows = grad.shape[0]
    tap_grads = [jnp.sum(grad * values, axis=0, keepdims=True)]
    total = taps[0:1, :] * grad
    for tap in range(1, taps.shape[0]):
        masked = jnp.where(position >= tap, grad, 0.0)
        moved = pltpu.roll(values, tap, 0)
        tap_grads.append(jnp.sum(masked * moved, axis=0, keepdims=True))
        total = total + taps[tap : tap + 1, :] * pltpu.roll(masked, rows - tap, 0)
    return tap_grads, jnp.sum(grad, axis=0, keepdims=True), total


def decay_of(mask, cum, cum_t, head):
    apart = cum[:, head : head + 1] - cum_t[head : head + 1, :]
    return jnp.exp(jnp.where(mask, apart, -1e30))


def per_lane(values, pair):
    rows = values.shape[0]
    low = iota((rows, 2 * HD), 1) < HD
    return jnp.where(
        low, values[:, 2 * pair : 2 * pair + 1], values[:, 2 * pair + 1 : 2 * pair + 2]
    )


def ssm_pieces(xs_ref, sk_ref, pos_ref, small_ref, ssmall_ref, head_ref, kcount):
    rows = xs_ref.shape[0]
    channels = small_ref.shape[1]
    states = ssmall_ref.shape[1]
    position = pos_ref[...]
    bias = slice(kcount, kcount + 1)
    x_pre = conv(xs_ref[:, :channels], small_ref[:kcount, :], small_ref[bias, :], position)
    state_pre = conv(sk_ref[:, :states], ssmall_ref[:kcount, :], ssmall_ref[bias, :], position)
    state_act = (state_pre * sigmoid(state_pre)).astype(bf16)
    b_matrix, c_matrix = state_act[:, : states // 2], state_act[:, states // 2 :]
    raw = xs_ref[:, channels:] + head_ref[0:1, :]
    step = jnp.maximum(raw, 0.0) + jnp.log1p(jnp.exp(-jnp.abs(raw)))
    paced = step * head_ref[1:2, :]
    row_at, col_at = iota((rows, rows), 0), iota((rows, rows), 1)
    upper = (row_at <= col_at).astype(f32)
    lower = (col_at <= row_at).astype(f32)
    cum = exact(lower, paced, ((1,), (0,)))
    cum_t = exact(paced, upper, ((0,), (0,)))
    gram = dot_nt(c_matrix, b_matrix)
    return x_pre, state_pre, b_matrix, c_matrix, raw, step, cum, cum_t, gram, upper


def ssm_forward_kernel(
    kcount, zq_ref, xs_ref, sk_ref, pos_ref, small_ref, ssmall_ref, head_ref, skip_ref, gated_ref
):
    rows, channels = gated_ref.shape
    x_pre, _, _, _, _, step, cum, cum_t, gram, _ = ssm_pieces(
        xs_ref, sk_ref, pos_ref, small_ref, ssmall_ref, head_ref, kcount
    )
    x_act = x_pre * sigmoid(x_pre)
    mask = segment_mask(pos_ref[...])
    low = iota((rows, 2 * HD), 1) < HD
    for pair in range(channels // (2 * HD)):
        lanes = slice(2 * HD * pair, 2 * HD * (pair + 1))
        act = x_act[:, lanes]
        drive = (per_lane(step, pair) * act).astype(bf16)
        outs = []
        for side in range(2):
            mix = (decay_of(mask, cum, cum_t, 2 * pair + side) * gram).astype(bf16)
            outs.append(dot(mix, drive))
        out = jnp.where(low, outs[0], outs[1]) + skip_ref[0:1, lanes] * act
        gate = zq_ref[:, lanes]
        gated_ref[:, lanes] = out * (gate * sigmoid(gate))


def attention_keys(sk_ref, cosine, sine):
    last = sk_ref.shape[1]
    key = sk_ref[:, last - 2 * AHD : last - AHD]
    key = (key * cosine + pltpu.roll(key, AHD // 2, 1) * sine).astype(bf16)
    return key, sk_ref[:, last - AHD :].astype(bf16)


def attention_head(zq_ref, first, head, key, mask, cosine, sine):
    query = zq_ref[:, first + AHD * head : first + AHD * (head + 1)]
    query = (query * cosine + pltpu.roll(query, AHD // 2, 1) * sine).astype(bf16)
    scores = dot_nt(query, key) * AHD ** (-0.5)
    weights = jnp.where(mask, jnp.exp(jnp.where(mask, scores, 0.0)), 0.0)
    return query, weights / jnp.sum(weights, axis=1, keepdims=True)


def attention_forward_kernel(zq_ref, sk_ref, pos_ref, cos_ref, sin_ref, ctx_ref):
    heads = ctx_ref.shape[1] // AHD
    first = zq_ref.shape[1] - heads * AHD
    cosine, sine = cos_ref[...], sin_ref[...]
    mask = segment_mask(pos_ref[...])
    key, value = attention_keys(sk_ref, cosine, sine)
    for head in range(heads):
        _, prob = attention_head(zq_ref, first, head, key, mask, cosine, sine)
        ctx_ref[:, AHD * head : AHD * (head + 1)] = dot(prob.astype(bf16), value).astype(bf16)


def attention_backward_kernel(
    zq_ref, sk_ref, pos_ref, cos_ref, sin_ref, back_ref, qgrad_ref, kvgrad_ref
):
    heads = qgrad_ref.shape[1] // AHD
    first = zq_ref.shape[1] - heads * AHD
    cosine, sine = cos_ref[...], sin_ref[...]
    mask = segment_mask(pos_ref[...])
    key, value = attention_keys(sk_ref, cosine, sine)

    def unrotate(grad):
        return grad * cosine - pltpu.roll(grad, AHD // 2, 1) * sine

    key_total = None
    value_total = None
    for head in range(heads):
        lanes = slice(AHD * head, AHD * (head + 1))
        back = back_ref[:, lanes].astype(bf16)
        query, prob = attention_head(zq_ref, first, head, key, mask, cosine, sine)
        value_part = dot_tn(prob.astype(bf16), back)
        prob_grad = dot_nt(back, value)
        delta = jnp.sum(prob * prob_grad, axis=1, keepdims=True)
        score_back = (prob * (prob_grad - delta) * AHD ** (-0.5)).astype(bf16)
        qgrad_ref[:, lanes] = unrotate(dot(score_back, key)).astype(bf16)
        key_part = dot_tn(score_back, query)
        key_total = key_part if head == 0 else key_total + key_part
        value_total = value_part if head == 0 else value_total + value_part
    kvgrad_ref[:, :AHD] = unrotate(key_total).astype(bf16)
    kvgrad_ref[:, AHD:] = value_total.astype(bf16)


def ssm_backward_kernel(
    kcount, sback_ref, gated_ref, scale_ref, zq_ref, xs_ref, sk_ref, pos_ref, small_ref,
    ssmall_ref, head_ref, skip_ref, zx_ref, stback_ref, wide_ref, state_ref, lane_ref,
):
    rows, channels = gated_ref.shape
    states = ssmall_ref.shape[1]
    position = pos_ref[...]
    mask = segment_mask(position)
    full_pre, state_pre, b_matrix, c_matrix, raw, step, cum, cum_t, gram, upper = ssm_pieces(
        xs_ref, sk_ref, pos_ref, small_ref, ssmall_ref, head_ref, kcount
    )
    scale, pull = scale_ref[:, 0:1], scale_ref[:, 1:2]
    width = step.shape[1]
    low = iota((rows, 2 * HD), 1) < HD
    lane = iota((rows, width), 1)
    line = iota((width, rows), 0)
    gram_back = jnp.zeros((rows, rows), f32)
    row_sums = jnp.zeros((rows, width), f32)
    col_sums = jnp.zeros((width, rows), f32)
    raw_back = jnp.zeros((rows, width), f32)
    wide_ref[...] = jnp.zeros_like(wide_ref)
    state_ref[...] = jnp.zeros_like(state_ref)
    lane_ref[...] = jnp.zeros_like(lane_ref)
    for pair in range(channels // (2 * HD)):
        lanes = slice(2 * HD * pair, 2 * HD * (pair + 1))
        back, gated = sback_ref[:, lanes], gated_ref[:, lanes]
        wide_ref[kcount + 1 : kcount + 2, lanes] = jnp.sum(
            back * gated * scale, axis=0, keepdims=True
        )
        gated_back = scale * (back * small_ref[kcount + 1 : kcount + 2, lanes]) - gated * pull
        gate = zq_ref[:, lanes]
        part = sigmoid(gate)
        out_back = gated_back * (gate * part)
        x_pre = full_pre[:, lanes]
        x_part = sigmoid(x_pre)
        act = x_pre * x_part
        wide_ref[kcount + 2 : kcount + 3, lanes] = jnp.sum(out_back * act, axis=0, keepdims=True)
        out_half = out_back.astype(bf16)
        drive = (per_lane(step, pair) * act).astype(bf16)
        backs = []
        outs = []
        for side in range(2):
            head = 2 * pair + side
            decay = decay_of(mask, cum, cum_t, head)
            mix = decay * gram
            mix_half = mix.astype(bf16)
            outs.append(dot(mix_half, drive))
            backs.append(dot_tn(mix_half, out_half))
            inside = low if side == 0 else jnp.logical_not(low)
            mine = jnp.where(inside, out_back, 0.0).astype(bf16)
            mix_back = dot_nt(mine, drive)
            gram_back = gram_back + mix_back * decay
            pairs = mix_back * mix
            row_sums = jnp.where(lane == head, jnp.sum(pairs, axis=1, keepdims=True), row_sums)
            col_sums = jnp.where(line == head, jnp.sum(pairs, axis=0, keepdims=True), col_sums)
        flat = jnp.where(low, outs[0], outs[1]) + skip_ref[0:1, lanes] * act
        zx_ref[:, lanes] = (gated_back * flat * (part * (1.0 + gate * (1.0 - part)))).astype(bf16)
        drive_back = jnp.where(low, backs[0], backs[1])
        product = drive_back * act
        for side in range(2):
            inside = low if side == 0 else jnp.logical_not(low)
            summed = jnp.sum(jnp.where(inside, product, 0.0), axis=1, keepdims=True)
            raw_back = jnp.where(lane == 2 * pair + side, summed, raw_back)
        act_back = skip_ref[0:1, lanes] * out_back + per_lane(step, pair) * drive_back
        pre_back = act_back * (x_part * (1.0 + x_pre * (1.0 - x_part)))
        tap_grads, bias_grad, x_back = conv_back(
            pre_back, xs_ref[:, lanes], small_ref[:kcount, lanes], position
        )
        for tap in range(kcount):
            wide_ref[tap : tap + 1, lanes] = tap_grads[tap]
        wide_ref[kcount : kcount + 1, lanes] = bias_grad
        zx_ref[:, channels + 2 * HD * pair : channels + 2 * HD * (pair + 1)] = x_back.astype(bf16)
    log_back = exact(upper, row_sums, ((1,), (0,))) - exact(upper, col_sums, ((1,), (1,)))
    rate = head_ref[1:2, :]
    raw_back = (raw_back + log_back * rate) * sigmoid(raw)
    zx_ref[:, 2 * channels :] = raw_back.astype(bf16)
    lane_ref[0:1, :] = jnp.sum(raw_back, axis=0, keepdims=True)
    lane_ref[1:2, :] = jnp.sum(log_back * step, axis=0, keepdims=True) * rate
    gram_half = gram_back.astype(bf16)
    state_part = sigmoid(state_pre)
    state_slope = state_part * (1.0 + state_pre * (1.0 - state_part))
    sides = (dot_tn(gram_half, c_matrix), dot(gram_half, b_matrix))
    for side in range(2):
        cols = slice(states // 2 * side, states // 2 * (side + 1))
        tap_grads, bias_grad, s_back = conv_back(
            sides[side] * state_slope[:, cols], sk_ref[:, cols], ssmall_ref[:kcount, cols], position
        )
        for tap in range(kcount):
            state_ref[tap : tap + 1, cols] = tap_grads[tap]
        state_ref[kcount : kcount + 1, cols] = bias_grad
        stback_ref[:, cols] = s_back.astype(bf16)


def project_kernel(
    tensor_count,
    ranks_ref, rows_ref, wzq0_ref, wzq1_ref, wxs0_ref, wxs1_ref, wide0_ref, wide1_ref, to_d_ref,
    to_g_ref, nat_ref, normed_ref, group_ref, zq_ref, xs_ref, sk_ref, wsk_ref, scale_ref,
    xsmall_ref, gains_ref, ssmall_ref,
):
    width = rows_ref.shape[1]
    half = width // 2
    places = wide0_ref.shape[0]
    shard = half // places

    def spread(at, extent, out_ref):
        count = 2 * places
        block = out_ref.shape[1] // extent
        small = block // count
        source, target = iota((128, out_ref.shape[1]), 0), iota((128, out_ref.shape[1]), 1)
        known = source < extent * small
        base = source // small * block + source % small
        total = jnp.zeros(out_ref.shape, f32)
        for place in range(count):
            wide_ref = wide0_ref if place < places else wide1_ref
            rows_of = wide_ref[place % places, shard : shard + 16, at : at + 128]
            hot = known & (target == base + ranks_ref[place] * small)
            total = total + dot(rows_of, hot.astype(bf16))
        out_ref[...] = total

    spread(0, xsmall_ref.shape[1] // HD, xsmall_ref)
    spread(128, tensor_count, gains_ref)
    spread(256, tensor_count, ssmall_ref)
    values = rows_ref[...].astype(f32)
    scale = lax.rsqrt(jnp.mean(values * values, axis=1, keepdims=True) + norm_eps)
    scale_ref[...] = scale
    nat = (values * scale * gains_ref[0:1, :]).astype(bf16)
    nat_ref[...] = nat
    normed = dot(nat, to_d_ref[...]).astype(bf16)
    normed_ref[...] = normed
    group_ref[...] = dot(nat, to_g_ref[...]).astype(bf16)
    first, second = normed[:, :half], normed[:, half:]
    zq_ref[...] = dot(first, wzq0_ref[...]) + dot(second, wzq1_ref[...])
    xs_ref[...] = dot(first, wxs0_ref[...]) + dot(second, wxs1_ref[...])
    wide0 = wide0_ref[:, :shard, :].reshape(half, wide0_ref.shape[2])
    wide1 = wide1_ref[:, :shard, :].reshape(half, wide1_ref.shape[2])
    wsk = (dot(to_g_ref[:, :half], wide0) + dot(to_g_ref[:, half:], wide1)).astype(bf16)
    wsk_ref[...] = wsk
    sk_ref[...] = dot(nat, wsk)


def pack_kernel(left_ref, right_ref, other_left_ref, other_right_ref, out_ref):
    cut = right_ref.shape[1]
    out_ref[:, :cut] = dot_tn(left_ref[...], right_ref[...]).astype(bf16)
    out_ref[:, cut:] = dot_tn(other_left_ref[...], other_right_ref[...]).astype(bf16)


def back_project_kernel(
    zx_ref, query_ref, sk_ref, wzq0_ref, wzq1_ref, wxs0_ref, wxs1_ref, wsk_ref, to_d_ref, rows_ref,
    scale_ref, out_ref, gain_ref,
):
    half = wsk_ref.shape[0] // 2
    channels = wzq0_ref.shape[1] - query_ref.shape[1]
    zq = jnp.concatenate([zx_ref[:, :channels], query_ref[...]], axis=1)
    xs = zx_ref[:, channels:]
    total = dot_nt(sk_ref[...], wsk_ref[...])
    for at, wzq_ref, wxs_ref in ((0, wzq0_ref, wxs0_ref), (half, wzq1_ref, wxs1_ref)):
        part = (dot_nt(zq, wzq_ref[...]) + dot_nt(xs, wxs_ref[...])).astype(bf16)
        total = total + dot_nt(part, to_d_ref[:, at : at + half])
    out_ref[...] = total.astype(bf16)
    gain_ref[...] = jnp.sum(
        total * rows_ref[...].astype(f32) * scale_ref[...], axis=0, keepdims=True
    )


def call(kernel, outs, flops, *args, scalars=0):
    moved = sum(item.size * item.dtype.itemsize for item in args)
    listed = outs if isinstance(outs, tuple) else (outs,)
    moved += sum(item.size * item.dtype.itemsize for item in listed)
    return pl.pallas_call(
        kernel,
        out_shape=outs,
        in_specs=[
            pl.BlockSpec(memory_space=pltpu.SMEM if at < scalars else pltpu.VMEM)
            for at in range(len(args))
        ],
        cost_estimate=pl.CostEstimate(flops=flops, bytes_accessed=moved, transcendentals=0),
        compiler_params=pltpu.CompilerParams(vmem_limit_bytes=24 << 20),
    )(*args)


def shape(dtype, *dims):
    return jax.ShapeDtypeStruct(dims, dtype)


class Ring:
    def __init__(self):
        self.count = lax.axis_size("dp")
        self.me = lax.axis_index("dp")
        bits = []
        bit = 2
        while bit < self.count:
            bits.append(bit)
            bit *= 2
        self.high_first = bits[::-1]
        self.orders = (bits, bits[::-1])

    def swap(self, value, bit):
        return lax.ppermute(value, "dp", [(i, i ^ bit) for i in range(self.count)])

    def rank_at(self, place):
        half = self.count // 2
        return self.me ^ ((place % half) * 2 + place // half)

    def gather(self, shard, kind):
        have = []
        value = shard
        lead = 0
        first = None
        for bit in self.orders[kind]:
            axis = sum(1 for other in have if other > bit)
            got = self.swap(value, bit)
            first = got if first is None else first
            value = jnp.stack([value, got], axis=axis)
            have.append(bit)
            lead += 1
        flat = (self.count // 2 * shard.shape[0],) + shard.shape[1:]
        return (value.reshape(flat), self.swap(value, 1).reshape(flat)), first

    def reduce(self, half_sum, kind):
        wire = half_sum.dtype
        levels = len(self.high_first)
        rest = (half_sum.shape[0] * 2 // self.count,) + half_sum.shape[1:]
        total = half_sum.astype(f32).reshape((2,) * levels + rest)
        left = list(self.high_first)
        for bit in self.orders[1 - kind]:
            axis = left.index(bit)
            keep = lax.index_in_dim(total, 0, axis, keepdims=False)
            send = lax.index_in_dim(total, 1, axis, keepdims=False).astype(wire)
            total = keep + self.swap(send, bit).astype(f32)
            left.remove(bit)
        return total


def turn(value, step):
    count = lax.axis_size("tensor")
    return lax.ppermute(value, "tensor", [(i, (i + step) % count) for i in range(count)])


def z_sum(value):
    total = value
    for step in range(1, lax.axis_size("tensor")):
        total = total + turn(value, step)
    return total


def z_scatter(value):
    count = lax.axis_size("tensor")
    rank = lax.axis_index("tensor")
    blocks = value.reshape((count, value.shape[0] // count) + value.shape[1:])

    def block(step):
        return lax.dynamic_index_in_dim(blocks, (rank + step) % count, 0, keepdims=False)

    got = [turn(block(step), step) for step in range(1, count)]
    total = block(0).astype(f32)
    for part in got:
        total = total + part.astype(f32)
    return total


def z_gather_async(value):
    count = lax.axis_size("tensor")
    rank = lax.axis_index("tensor")
    whole = jnp.zeros((count,) + value.shape, value.dtype)
    whole = lax.dynamic_update_index_in_dim(whole, value, rank, 0)
    for step in range(1, count):
        whole = lax.dynamic_update_index_in_dim(
            whole, turn(value, step), (rank - step) % count, 0
        )
    return whole.reshape((count * value.shape[0],) + value.shape[1:])


def z_gather(value):
    return lax.all_gather(value, "tensor", axis=0, tiled=True)


def local(
    block_input,
    positions,
    out_grad,
    in_gain,
    z_proj,
    x_proj,
    step_proj,
    state_proj,
    x_conv,
    x_conv_bias,
    state_conv,
    state_conv_bias,
    decay_log,
    step_bias,
    skip_gain,
    mixer_gain,
    mixer_out,
    query_proj,
    keyval_proj,
    attn_out,
    ffn_gain,
    gate_proj,
    up_proj,
    down_proj,
):
    ring = Ring()
    n = ring.count
    tensor = lax.axis_size("tensor")
    rank = lax.axis_index("tensor")
    width = block_input.shape[1]
    own_rows = block_input.shape[0]
    rows = own_rows * tensor
    heads = decay_log.shape[0]
    channels = heads * HD
    all_channels = channels * tensor
    shard = width // n
    piece = width // (n * tensor)
    kcount = x_conv.shape[0]
    q_local = query_proj.shape[1] // AHD
    group_size = q_local * tensor // KVH
    kv_head = rank * q_local // group_size
    state_width = 2 * NSTATE

    step_pad = (-heads) % 128
    inner = HD // n
    state_inner = state_width // (n * tensor)
    pack_width = state_width + keyval_proj.shape[1]
    shared_small = jnp.concatenate(
        [
            jnp.pad(jnp.stack([in_gain, ffn_gain]), ((0, kcount - 1), (0, 0))),
            jnp.concatenate([state_conv, state_conv_bias[None]], axis=0),
        ],
        axis=1,
    )
    shared_small = jnp.pad(
        shared_small, ((0, 15 - kcount), (0, pack_width - shared_small.shape[1]))
    )
    joined = jnp.concatenate(
        [jnp.concatenate([state_proj, keyval_proj], axis=1), shared_small], axis=0
    )
    own_small = jnp.concatenate([x_conv, x_conv_bias[None], mixer_gain[None]], axis=0)
    own_small = own_small.reshape(kcount + 2, heads * inner)
    joined = z_gather_async(joined).reshape(tensor, -1, pack_width)

    wzq, first_a = ring.gather(jnp.concatenate([z_proj, query_proj], axis=1), 0)
    wxs, first_b = ring.gather(
        jnp.concatenate([x_proj, jnp.pad(step_proj, ((0, 0), (0, step_pad)))], axis=1), 1
    )
    rows_nat = z_gather_async(block_input)
    shared = joined[:, :piece].reshape(shard, pack_width)
    small_at = state_width + 2 * AHD
    small_rows = joined[:, piece:]
    gain_cols = small_rows[:, :, :piece].transpose(1, 0, 2).reshape(16, -1)
    state_cols = small_rows[:, :, piece : piece + state_inner].transpose(1, 0, 2).reshape(16, -1)
    small_block = jnp.concatenate(
        [
            jnp.pad(own_small, ((0, 14 - kcount), (0, 128 - heads * inner))),
            jnp.pad(gain_cols, ((0, 0), (0, 128 - gain_cols.shape[1]))),
            jnp.pad(state_cols, ((0, 0), (0, small_at - 256 - state_cols.shape[1]))),
        ],
        axis=1,
    )
    wide = jnp.concatenate(
        [
            shared[:, :state_width],
            lax.dynamic_slice_in_dim(shared, state_width + kv_head * AHD, AHD, 1),
            lax.dynamic_slice_in_dim(shared, state_width + KVH * AHD + kv_head * AHD, AHD, 1),
        ],
        axis=1,
    )
    wide = jnp.concatenate([wide, small_block], axis=0)
    wide_parts, _ = ring.gather(wide, 1)
    wide_parts = [part.reshape(n // 2, -1, small_at) for part in wide_parts]

    late = lax.optimization_barrier((mixer_out, attn_out, gate_proj, up_proj, down_proj, wide))
    late = jnp.concatenate([late[0].T, late[1].T, late[2], late[3], late[4].T], axis=1)
    late_all = lax.all_gather(late, "dp", axis=0, tiled=True)
    cuts = [0]
    for item in (mixer_out.shape[0], attn_out.shape[0], gate_proj.shape[1], up_proj.shape[1], down_proj.shape[0]):
        cuts.append(cuts[-1] + item)
    w_mix, w_attn, w_gate, w_up, w_down = (
        late_all[:, cuts[i] : cuts[i + 1]] for i in range(5)
    )
    w_gu = late_all[:, cuts[2] : cuts[4]]
    ffl = gate_proj.shape[1]

    ranks = jnp.arange(n)
    pick = (ring.rank_at(ranks)[:, None] == ranks[None, :]).astype(f32)
    place = jnp.arange(width)
    feature_d = ring.rank_at(place // shard) * shard + place % shard
    inside = place % shard
    feature_g = (
        inside // piece * (width // tensor) + ring.rank_at(place // shard) * piece + inside % piece
    )
    to_d = (place[:, None] == feature_d[None, :]).astype(bf16)
    to_g = (place[:, None] == feature_g[None, :]).astype(bf16)
    half = width // 2
    own_resid = block_input.astype(f32)
    small_width = small_at
    (
        normed_nat, normed, normed_g, zq_lin, xs_lin, sk_lin, w_sk, in_scale, x_small, gains_all,
        state_small_in,
    ) = call(
        functools.partial(project_kernel, tensor),
        (
            shape(bf16, rows, width),
            shape(bf16, rows, width),
            shape(bf16, rows, width),
            shape(f32, rows, wzq[0].shape[1]),
            shape(f32, rows, wxs[0].shape[1]),
            shape(f32, rows, small_width),
            shape(bf16, width, small_width),
            shape(f32, rows, 1),
            shape(f32, 16, channels),
            shape(f32, 16, width),
            shape(f32, 16, state_width),
        ),
        4 * 10**9,
        ring.rank_at(ranks), rows_nat, *wzq, *wxs, *wide_parts, to_d, to_g,
        scalars=1,
    )
    in_gain_f, ffn_gain_f = gains_all[0], gains_all[1]
    mixer_gain_f = x_small[kcount + 1]
    grad_all = z_gather_async(lax.optimization_barrier((out_grad, zq_lin))[0])
    position = positions.reshape(rows, 1)
    decay_rate = -jnp.exp(decay_log)
    lanes_pad = (0, step_pad)
    head_rows = jnp.stack([jnp.pad(step_bias, lanes_pad), jnp.pad(decay_rate, lanes_pad)])
    skip_row = jnp.repeat(skip_gain, HD)[None]
    step_width = heads + step_pad
    ssm_params = (position, x_small, state_small_in, head_rows, skip_row)
    gated_out = call(
        functools.partial(ssm_forward_kernel, kcount),
        shape(f32, rows, channels),
        2 * 10**9,
        zq_lin, xs_lin, sk_lin, *ssm_params,
    )
    square_sums = z_sum(jnp.sum(gated_out * gated_out, axis=1))
    freq_rates = rope_base ** (-2.0 * jnp.arange(AHD // 2, dtype=f32) / AHD)
    angles = positions.astype(f32)[:, None] * freq_rates[None, :]
    cosine, sine = jnp.cos(angles), jnp.sin(angles)
    cosine = jnp.concatenate([cosine, cosine], axis=1)
    sine = jnp.concatenate([-sine, sine], axis=1)
    context = call(
        attention_forward_kernel,
        shape(bf16, rows, q_local * AHD),
        2 * 10**9,
        zq_lin, sk_lin, position, cosine, sine,
    )
    ssm_scale = lax.rsqrt(square_sums / all_channels + norm_eps)[:, None]
    ssm_normed = (gated_out * ssm_scale * mixer_gain_f[None, :]).astype(bf16)

    mixed = z_scatter((dot_nt(ssm_normed, w_mix) + dot_nt(context, w_attn)).astype(bf16))
    hidden = own_resid + mixed
    ff_scale = lax.rsqrt(jnp.mean(hidden * hidden, axis=1, keepdims=True) + norm_eps)
    ffn_in = z_gather((hidden * ff_scale * ffn_gain_f[None, :]).astype(bf16))

    gu_lin = dot(ffn_in, w_gu)
    gate_lin, up_lin = gu_lin[:, :ffl], gu_lin[:, ffl:]
    gate_act = jax.nn.silu(gate_lin)
    ffn_act = (gate_act * up_lin).astype(bf16)
    act_grad = dot(grad_all, w_down)
    gate_back = (act_grad * up_lin * silu_grad(gate_lin)).astype(bf16)
    up_back = (act_grad * gate_act).astype(bf16)
    gu_back = jnp.concatenate([gate_back, up_back], axis=1)
    ffn_pack = call(
        pack_kernel,
        shape(bf16, width, 3 * ffl),
        3 * 10**9,
        ffn_in, gu_back, grad_all, ffn_act,
    )
    ffn_back = z_scatter(dot_nt(gu_back, w_gu).astype(bf16))
    ffn_back, ffn_pack = lax.optimization_barrier((ffn_back, ffn_pack))
    ffn_gain_part = jnp.sum(ffn_back * hidden * ff_scale, axis=0)
    ffn_norm_back = ffn_back * ffn_gain_f[None, :]
    resid_grad = (
        out_grad.astype(f32)
        + ff_scale * ffn_norm_back
        - hidden * ff_scale**3 * jnp.mean(ffn_norm_back * hidden, axis=1, keepdims=True)
    )
    resid_all = z_gather(resid_grad.astype(bf16))
    ffn_red = lax.psum_scatter(ffn_pack, "dp", scatter_dimension=0, tiled=True).astype(f32)
    ffn_rows = z_scatter(
        lax.optimization_barrier((dot_nt(ffn_act, w_down).astype(bf16), resid_all))[0]
    )
    output = (hidden + ffn_rows).astype(bf16)

    ssm_back = dot(resid_all, w_mix)
    ctx_back = dot(resid_all, w_attn)
    row_dots = z_sum(jnp.sum(ssm_back * mixer_gain_f[None, :] * gated_out, axis=1))
    query_grad, kv_grad = call(
        attention_backward_kernel,
        (shape(bf16, rows, q_local * AHD), shape(bf16, rows, 2 * AHD)),
        2 * 10**9,
        zq_lin, sk_lin, position, cosine, sine, ctx_back,
    )
    mid_pack = call(
        pack_kernel,
        shape(bf16, width, channels + 2 * q_local * AHD),
        2 * 10**9,
        resid_all, jnp.concatenate([ssm_normed, context], axis=1), normed_nat, query_grad,
    )
    row_dots, mid_pack, ffn_red = lax.optimization_barrier((row_dots, mid_pack, ffn_red))
    mid_red = lax.psum_scatter(mid_pack, "dp", scatter_dimension=0, tiled=True).astype(f32)
    qwide = q_local * AHD
    mixer_red = mid_red[:, :channels].T
    attn_red = mid_red[:, channels : channels + qwide].T
    query_red = mid_red[:, channels + qwide :]
    pull = ssm_scale**3 * row_dots[:, None] / all_channels
    zx_half, state_half, wide_sums, state_sums, lane_sums = call(
        functools.partial(ssm_backward_kernel, kcount),
        (
            shape(bf16, rows, 2 * channels + step_width),
            shape(bf16, rows, state_width),
            shape(f32, kcount + 4, channels),
            shape(f32, kcount + 4, state_width),
            shape(f32, 8, step_width),
        ),
        4 * 10**9,
        ssm_back, gated_out, jnp.concatenate([ssm_scale, pull], axis=1),
        zq_lin, xs_lin, sk_lin, *ssm_params,
    )
    x_taps_grad = wide_sums[:kcount]
    x_bias_grad = wide_sums[kcount]
    mixer_gain_grad = wide_sums[kcount + 1]
    skip_grad = jnp.sum(wide_sums[kcount + 2].reshape(heads, HD), axis=1)
    step_bias_grad = lane_sums[0, :heads]
    decay_log_grad = lane_sums[1, :heads]
    sk_half = jnp.concatenate([state_half, kv_grad], axis=1)
    zx_send = dot_tn(normed[:, half:], zx_half).astype(bf16)
    sk_send = dot_tn(normed_g[:, half:], sk_half).astype(bf16)
    zx_sum = dot_tn(normed[:, :half], zx_half) + ring.swap(zx_send, 1).astype(f32)
    sk_sum = dot_tn(normed_g[:, :half], sk_half) + ring.swap(sk_send, 1).astype(f32)
    zx_in, sk_in, zx_sum, sk_sum = lax.optimization_barrier(
        (zx_half, sk_half, zx_sum.astype(bf16), sk_sum.astype(bf16))
    )
    normed_back, in_gain_sum = call(
        back_project_kernel,
        (shape(bf16, rows, width), shape(f32, 1, width)),
        3 * 10**9,
        zx_in, query_grad, sk_in, *wzq, *wxs, w_sk, to_d, rows_nat, in_scale,
    )
    zx_red = ring.reduce(zx_sum, 1)
    sk_red = ring.reduce(sk_sum, 0)
    normed_back_own = z_scatter(normed_back)
    gate_red = ffn_red[:, :ffl]
    up_red = ffn_red[:, ffl : 2 * ffl]
    down_red = ffn_red[:, 2 * ffl :].T
    z_red = zx_red[:, :channels]
    xs_red = zx_red[:, channels:]

    own_in_scale = lax.rsqrt(jnp.mean(own_resid * own_resid, axis=1, keepdims=True) + norm_eps)
    gains = jnp.stack([in_gain_sum[0], ffn_gain_part])

    def by_rank(value):
        lead = value.size // HD
        return value.reshape(lead, n, inner).transpose(1, 0, 2).reshape(n, lead * inner)

    head_terms = jnp.concatenate([decay_log_grad, step_bias_grad, skip_grad])
    state_small = state_sums[: kcount + 1]
    per_rank = [
        by_rank(x_taps_grad),
        by_rank(x_bias_grad),
        by_rank(mixer_gain_grad),
        jnp.broadcast_to(head_terms[None], (n, 3 * heads)),
    ]
    per_both = jnp.concatenate(
        [
            gains.reshape(2, tensor, n, piece).transpose(2, 1, 0, 3).reshape(n, tensor, -1),
            state_small.reshape(kcount + 1, tensor, n, state_inner)
            .transpose(2, 1, 0, 3)
            .reshape(n, tensor, -1),
        ],
        axis=2,
    )
    both_size = per_both.shape[2]
    flat = jnp.concatenate(per_rank + [per_both.reshape(n, -1)], axis=1)
    flat = jnp.dot(pick, flat, precision=HIGHEST)
    flat_red = ring.reduce(flat[: n // 2] + ring.swap(flat[n // 2 :], 1), 0)[0]
    parts = []
    at = 0
    for item in per_rank:
        parts.append(flat_red[at : at + item.shape[1]])
        at += item.shape[1]
    x_taps_red = parts[0].reshape(kcount, heads, inner)
    x_bias_red = parts[1].reshape(heads, inner)
    mixer_gain_red = parts[2].reshape(heads, inner)
    heads_red = parts[3].reshape(3, heads)
    sk_blocks = sk_red.astype(bf16).reshape(tensor, piece, -1)
    both_rows = flat_red[at:].astype(bf16).reshape(tensor, 1, both_size)
    both_rows = jnp.pad(both_rows, ((0, 0), (0, 15), (0, sk_blocks.shape[2] - both_size)))
    sk_blocks = jnp.concatenate([sk_blocks, both_rows], axis=1)
    both_red = jnp.zeros((both_size,), f32)
    state_own = jnp.zeros((piece, state_width), f32)
    key_cols = [jnp.zeros((piece, AHD), f32) for _ in range(KVH)]
    value_cols = [jnp.zeros((piece, AHD), f32) for _ in range(KVH)]
    for step in range(tensor):
        sent = lax.dynamic_index_in_dim(sk_blocks, (rank + step) % tensor, 0, keepdims=False)
        got = (turn(sent, step) if step else sent).astype(f32)
        both_red = both_red + got[piece, :both_size]
        got = got[:piece]
        head_of = (rank - step) % tensor * q_local // group_size
        state_own = state_own + got[:, :state_width]
        for head in range(KVH):
            term = jnp.where(head_of == head, got[:, state_width:], 0.0)
            key_cols[head] = key_cols[head] + term[:, :AHD]
            value_cols[head] = value_cols[head] + term[:, AHD:]
    keyval_red = jnp.concatenate(key_cols + value_cols, axis=1)
    in_gain_red = both_red[:piece]
    ffn_gain_red = both_red[piece : 2 * piece]
    state_small_red = both_red[2 * piece :].reshape(kcount + 1, state_inner)

    in_back = normed_back_own * in_gain_f[None, :]
    input_grad = (
        resid_grad
        + own_in_scale * in_back
        - own_resid * own_in_scale**3 * jnp.mean(in_back * own_resid, axis=1, keepdims=True)
    )
    return (
        output,
        input_grad,
        in_gain_red,
        z_red,
        xs_red[:, :channels],
        xs_red[:, channels : channels + heads],
        state_own,
        x_taps_red,
        x_bias_red,
        state_small_red[:kcount],
        state_small_red[kcount],
        heads_red[0],
        heads_red[1],
        heads_red[2],
        mixer_gain_red,
        mixer_red,
        query_red,
        keyval_red,
        attn_red,
        ffn_gain_red,
        gate_red,
        up_red,
        down_red,
    )


def solution(mesh):
    in_specs = (
        P(("dp", "tensor"), None),
        P("dp"),
        P(("dp", "tensor"), None),
        P(("tensor", "dp")),
        P("dp", "tensor"),
        P("dp", "tensor"),
        P("dp", "tensor"),
        P(("tensor", "dp"), None),
        P(None, "tensor", "dp"),
        P("tensor", "dp"),
        P(None, ("tensor", "dp")),
        P(("tensor", "dp")),
        P("tensor"),
        P("tensor"),
        P("tensor"),
        P("tensor", "dp"),
        P("tensor", "dp"),
        P("dp", "tensor"),
        P(("tensor", "dp"), None),
        P("tensor", "dp"),
        P(("tensor", "dp")),
        P("dp", "tensor"),
        P("dp", "tensor"),
        P("tensor", "dp"),
    )
    out_specs = (
        P(("dp", "tensor"), None),
        P(("dp", "tensor"), None),
        P(("tensor", "dp")),
        P("dp", "tensor"),
        P("dp", "tensor"),
        P("dp", "tensor"),
        P(("tensor", "dp"), None),
        P(None, "tensor", "dp"),
        P("tensor", "dp"),
        P(None, ("tensor", "dp")),
        P(("tensor", "dp")),
        P("tensor"),
        P("tensor"),
        P("tensor"),
        P("tensor", "dp"),
        P("tensor", "dp"),
        P("dp", "tensor"),
        P(("tensor", "dp"), None),
        P("tensor", "dp"),
        P(("tensor", "dp")),
        P("dp", "tensor"),
        P("dp", "tensor"),
        P("tensor", "dp"),
    )
    return jax.shard_map(local, mesh=mesh, in_specs=in_specs, out_specs=out_specs, check_vma=False)
```

```python
import functools

import jax
import jax.numpy as jnp
from jax import lax
from jax.experimental import pallas as pl
from jax.experimental.pallas import tpu as pltpu
from jax.sharding import PartitionSpec as P

HD = 64
NSTATE = 128
KVH = 2
AHD = 128

norm_eps = 1e-05
rope_base = 10000.0
bf16 = jnp.bfloat16
f32 = jnp.float32
HIGHEST = lax.Precision.HIGHEST


def dot(left, right):
    return jnp.dot(left, right, preferred_element_type=f32)


def dot_nt(left, right):
    return lax.dot_general(left, right, (((1,), (1,)), ((), ())), preferred_element_type=f32)


def dot_tn(left, right):
    return lax.dot_general(left, right, (((0,), (0,)), ((), ())), preferred_element_type=f32)


def sigmoid(values):
    return 1.0 / (1.0 + jnp.exp(-values))


def silu_grad(values):
    part = sigmoid(values)
    return part * (1.0 + values * (1.0 - part))


def exact(left, right, dims):
    return lax.dot_general(
        left, right, (dims, ((), ())), precision=HIGHEST, preferred_element_type=f32
    )


def iota(shape, axis):
    return lax.broadcasted_iota(jnp.int32, shape, axis)


def segment_mask(position):
    rows = position.shape[0]
    row_at, col_at = iota((rows, rows), 0), iota((rows, rows), 1)
    return (col_at <= row_at) & (col_at >= row_at - position)


def conv(values, taps, bias, position):
    total = bias + taps[0:1, :] * values
    for tap in range(1, taps.shape[0]):
        moved = jnp.where(position >= tap, pltpu.roll(values, tap, 0), 0.0)
        total = total + taps[tap : tap + 1, :] * moved
    return total


def conv_back(grad, values, taps, position):
    rows = grad.shape[0]
    tap_grads = [jnp.sum(grad * values, axis=0, keepdims=True)]
    total = taps[0:1, :] * grad
    for tap in range(1, taps.shape[0]):
        masked = jnp.where(position >= tap, grad, 0.0)
        moved = pltpu.roll(values, tap, 0)
        tap_grads.append(jnp.sum(masked * moved, axis=0, keepdims=True))
        total = total + taps[tap : tap + 1, :] * pltpu.roll(masked, rows - tap, 0)
    return tap_grads, jnp.sum(grad, axis=0, keepdims=True), total


def decay_of(mask, cum, cum_t, head):
    apart = cum[:, head : head + 1] - cum_t[head : head + 1, :]
    return jnp.exp(jnp.where(mask, apart, -1e30))


def per_lane(values, pair):
    rows = values.shape[0]
    low = iota((rows, 2 * HD), 1) < HD
    return jnp.where(
        low, values[:, 2 * pair : 2 * pair + 1], values[:, 2 * pair + 1 : 2 * pair + 2]
    )


def ssm_pieces(xs_ref, sk_ref, pos_ref, small_ref, ssmall_ref, head_ref, kcount):
    rows = xs_ref.shape[0]
    channels = small_ref.shape[1]
    states = ssmall_ref.shape[1]
    position = pos_ref[...]
    bias = slice(kcount, kcount + 1)
    x_pre = conv(xs_ref[:, :channels], small_ref[:kcount, :], small_ref[bias, :], position)
    state_pre = conv(sk_ref[:, :states], ssmall_ref[:kcount, :], ssmall_ref[bias, :], position)
    state_act = (state_pre * sigmoid(state_pre)).astype(bf16)
    b_matrix, c_matrix = state_act[:, : states // 2], state_act[:, states // 2 :]
    raw = xs_ref[:, channels:] + head_ref[0:1, :]
    step = jnp.maximum(raw, 0.0) + jnp.log1p(jnp.exp(-jnp.abs(raw)))
    paced = step * head_ref[1:2, :]
    row_at, col_at = iota((rows, rows), 0), iota((rows, rows), 1)
    upper = (row_at <= col_at).astype(f32)
    lower = (col_at <= row_at).astype(f32)
    cum = exact(lower, paced, ((1,), (0,)))
    cum_t = exact(paced, upper, ((0,), (0,)))
    gram = dot_nt(c_matrix, b_matrix)
    return x_pre, state_pre, b_matrix, c_matrix, raw, step, cum, cum_t, gram, upper


def ssm_forward_kernel(
    kcount, zq_ref, xs_ref, sk_ref, pos_ref, small_ref, ssmall_ref, head_ref, skip_ref, gated_ref
):
    rows, channels = gated_ref.shape
    x_pre, _, _, _, _, step, cum, cum_t, gram, _ = ssm_pieces(
        xs_ref, sk_ref, pos_ref, small_ref, ssmall_ref, head_ref, kcount
    )
    x_act = x_pre * sigmoid(x_pre)
    mask = segment_mask(pos_ref[...])
    low = iota((rows, 2 * HD), 1) < HD
    for pair in range(channels // (2 * HD)):
        lanes = slice(2 * HD * pair, 2 * HD * (pair + 1))
        act = x_act[:, lanes]
        drive = (per_lane(step, pair) * act).astype(bf16)
        outs = []
        for side in range(2):
            mix = (decay_of(mask, cum, cum_t, 2 * pair + side) * gram).astype(bf16)
            outs.append(dot(mix, drive))
        out = jnp.where(low, outs[0], outs[1]) + skip_ref[0:1, lanes] * act
        gate = zq_ref[:, lanes]
        gated_ref[:, lanes] = out * (gate * sigmoid(gate))


def attention_keys(sk_ref, cosine, sine):
    last = sk_ref.shape[1]
    key = sk_ref[:, last - 2 * AHD : last - AHD]
    key = (key * cosine + pltpu.roll(key, AHD // 2, 1) * sine).astype(bf16)
    return key, sk_ref[:, last - AHD :].astype(bf16)


def attention_head(zq_ref, first, head, key, mask, cosine, sine):
    query = zq_ref[:, first + AHD * head : first + AHD * (head + 1)]
    query = (query * cosine + pltpu.roll(query, AHD // 2, 1) * sine).astype(bf16)
    scores = dot_nt(query, key) * AHD ** (-0.5)
    weights = jnp.where(mask, jnp.exp(jnp.where(mask, scores, 0.0)), 0.0)
    return query, weights / jnp.sum(weights, axis=1, keepdims=True)


def attention_forward_kernel(zq_ref, sk_ref, pos_ref, cos_ref, sin_ref, ctx_ref):
    heads = ctx_ref.shape[1] // AHD
    first = zq_ref.shape[1] - heads * AHD
    cosine, sine = cos_ref[...], sin_ref[...]
    mask = segment_mask(pos_ref[...])
    key, value = attention_keys(sk_ref, cosine, sine)
    for head in range(heads):
        _, prob = attention_head(zq_ref, first, head, key, mask, cosine, sine)
        ctx_ref[:, AHD * head : AHD * (head + 1)] = dot(prob.astype(bf16), value).astype(bf16)


def attention_backward_kernel(
    zq_ref, sk_ref, pos_ref, cos_ref, sin_ref, back_ref, qgrad_ref, kvgrad_ref
):
    heads = qgrad_ref.shape[1] // AHD
    first = zq_ref.shape[1] - heads * AHD
    cosine, sine = cos_ref[...], sin_ref[...]
    mask = segment_mask(pos_ref[...])
    key, value = attention_keys(sk_ref, cosine, sine)

    def unrotate(grad):
        return grad * cosine - pltpu.roll(grad, AHD // 2, 1) * sine

    key_total = None
    value_total = None
    for head in range(heads):
        lanes = slice(AHD * head, AHD * (head + 1))
        back = back_ref[:, lanes].astype(bf16)
        query, prob = attention_head(zq_ref, first, head, key, mask, cosine, sine)
        value_part = dot_tn(prob.astype(bf16), back)
        prob_grad = dot_nt(back, value)
        delta = jnp.sum(prob * prob_grad, axis=1, keepdims=True)
        score_back = (prob * (prob_grad - delta) * AHD ** (-0.5)).astype(bf16)
        qgrad_ref[:, lanes] = unrotate(dot(score_back, key)).astype(bf16)
        key_part = dot_tn(score_back, query)
        key_total = key_part if head == 0 else key_total + key_part
        value_total = value_part if head == 0 else value_total + value_part
    kvgrad_ref[:, :AHD] = unrotate(key_total).astype(bf16)
    kvgrad_ref[:, AHD:] = value_total.astype(bf16)


def ssm_backward_kernel(
    kcount, sback_ref, gated_ref, scale_ref, zq_ref, xs_ref, sk_ref, pos_ref, small_ref,
    ssmall_ref, head_ref, skip_ref, zx_ref, stback_ref, wide_ref, state_ref, lane_ref,
):
    rows, channels = gated_ref.shape
    states = ssmall_ref.shape[1]
    position = pos_ref[...]
    mask = segment_mask(position)
    full_pre, state_pre, b_matrix, c_matrix, raw, step, cum, cum_t, gram, upper = ssm_pieces(
        xs_ref, sk_ref, pos_ref, small_ref, ssmall_ref, head_ref, kcount
    )
    scale, pull = scale_ref[:, 0:1], scale_ref[:, 1:2]
    width = step.shape[1]
    low = iota((rows, 2 * HD), 1) < HD
    lane = iota((rows, width), 1)
    line = iota((width, rows), 0)
    gram_back = jnp.zeros((rows, rows), f32)
    row_sums = jnp.zeros((rows, width), f32)
    col_sums = jnp.zeros((width, rows), f32)
    raw_back = jnp.zeros((rows, width), f32)
    wide_ref[...] = jnp.zeros_like(wide_ref)
    state_ref[...] = jnp.zeros_like(state_ref)
    lane_ref[...] = jnp.zeros_like(lane_ref)
    for pair in range(channels // (2 * HD)):
        lanes = slice(2 * HD * pair, 2 * HD * (pair + 1))
        back, gated = sback_ref[:, lanes], gated_ref[:, lanes]
        wide_ref[kcount + 1 : kcount + 2, lanes] = jnp.sum(
            back * gated * scale, axis=0, keepdims=True
        )
        gated_back = scale * (back * small_ref[kcount + 1 : kcount + 2, lanes]) - gated * pull
        gate = zq_ref[:, lanes]
        part = sigmoid(gate)
        out_back = gated_back * (gate * part)
        x_pre = full_pre[:, lanes]
        x_part = sigmoid(x_pre)
        act = x_pre * x_part
        wide_ref[kcount + 2 : kcount + 3, lanes] = jnp.sum(out_back * act, axis=0, keepdims=True)
        out_half = out_back.astype(bf16)
        drive = (per_lane(step, pair) * act).astype(bf16)
        backs = []
        outs = []
        for side in range(2):
            head = 2 * pair + side
            decay = decay_of(mask, cum, cum_t, head)
            mix = decay * gram
            mix_half = mix.astype(bf16)
            outs.append(dot(mix_half, drive))
            backs.append(dot_tn(mix_half, out_half))
            inside = low if side == 0 else jnp.logical_not(low)
            mine = jnp.where(inside, out_back, 0.0).astype(bf16)
            mix_back = dot_nt(mine, drive)
            gram_back = gram_back + mix_back * decay
            pairs = mix_back * mix
            row_sums = jnp.where(lane == head, jnp.sum(pairs, axis=1, keepdims=True), row_sums)
            col_sums = jnp.where(line == head, jnp.sum(pairs, axis=0, keepdims=True), col_sums)
        flat = jnp.where(low, outs[0], outs[1]) + skip_ref[0:1, lanes] * act
        zx_ref[:, lanes] = (gated_back * flat * (part * (1.0 + gate * (1.0 - part)))).astype(bf16)
        drive_back = jnp.where(low, backs[0], backs[1])
        product = drive_back * act
        for side in range(2):
            inside = low if side == 0 else jnp.logical_not(low)
            summed = jnp.sum(jnp.where(inside, product, 0.0), axis=1, keepdims=True)
            raw_back = jnp.where(lane == 2 * pair + side, summed, raw_back)
        act_back = skip_ref[0:1, lanes] * out_back + per_lane(step, pair) * drive_back
        pre_back = act_back * (x_part * (1.0 + x_pre * (1.0 - x_part)))
        tap_grads, bias_grad, x_back = conv_back(
            pre_back, xs_ref[:, lanes], small_ref[:kcount, lanes], position
        )
        for tap in range(kcount):
            wide_ref[tap : tap + 1, lanes] = tap_grads[tap]
        wide_ref[kcount : kcount + 1, lanes] = bias_grad
        zx_ref[:, channels + 2 * HD * pair : channels + 2 * HD * (pair + 1)] = x_back.astype(bf16)
    log_back = exact(upper, row_sums, ((1,), (0,))) - exact(upper, col_sums, ((1,), (1,)))
    rate = head_ref[1:2, :]
    raw_back = (raw_back + log_back * rate) * sigmoid(raw)
    zx_ref[:, 2 * channels :] = raw_back.astype(bf16)
    lane_ref[0:1, :] = jnp.sum(raw_back, axis=0, keepdims=True)
    lane_ref[1:2, :] = jnp.sum(log_back * step, axis=0, keepdims=True) * rate
    gram_half = gram_back.astype(bf16)
    state_part = sigmoid(state_pre)
    state_slope = state_part * (1.0 + state_pre * (1.0 - state_part))
    sides = (dot_tn(gram_half, c_matrix), dot(gram_half, b_matrix))
    for side in range(2):
        cols = slice(states // 2 * side, states // 2 * (side + 1))
        tap_grads, bias_grad, s_back = conv_back(
            sides[side] * state_slope[:, cols], sk_ref[:, cols], ssmall_ref[:kcount, cols], position
        )
        for tap in range(kcount):
            state_ref[tap : tap + 1, cols] = tap_grads[tap]
        state_ref[kcount : kcount + 1, cols] = bias_grad
        stback_ref[:, cols] = s_back.astype(bf16)


def project_kernel(
    tensor_count,
    ranks_ref, rows_ref, wzq0_ref, wzq1_ref, wxs0_ref, wxs1_ref, wide0_ref, wide1_ref, to_d_ref,
    to_g_ref, nat_ref, normed_ref, group_ref, zq_ref, xs_ref, sk_ref, wsk_ref, scale_ref,
    xsmall_ref, gains_ref, ssmall_ref,
):
    width = rows_ref.shape[1]
    half = width // 2
    places = wide0_ref.shape[0]
    shard = half // places

    def spread(at, extent, out_ref):
        count = 2 * places
        block = out_ref.shape[1] // extent
        small = block // count
        source, target = iota((128, out_ref.shape[1]), 0), iota((128, out_ref.shape[1]), 1)
        known = source < extent * small
        base = source // small * block + source % small
        total = jnp.zeros(out_ref.shape, f32)
        for place in range(count):
            wide_ref = wide0_ref if place < places else wide1_ref
            rows_of = wide_ref[place % places, shard : shard + 16, at : at + 128]
            hot = known & (target == base + ranks_ref[place] * small)
            total = total + dot(rows_of, hot.astype(bf16))
        out_ref[...] = total

    spread(0, xsmall_ref.shape[1] // HD, xsmall_ref)
    spread(128, tensor_count, gains_ref)
    spread(256, tensor_count, ssmall_ref)
    values = rows_ref[...].astype(f32)
    scale = lax.rsqrt(jnp.mean(values * values, axis=1, keepdims=True) + norm_eps)
    scale_ref[...] = scale
    nat = (values * scale * gains_ref[0:1, :]).astype(bf16)
    nat_ref[...] = nat
    normed = dot(nat, to_d_ref[...]).astype(bf16)
    normed_ref[...] = normed
    group_ref[...] = dot(nat, to_g_ref[...]).astype(bf16)
    first, second = normed[:, :half], normed[:, half:]
    zq_ref[...] = dot(first, wzq0_ref[...]) + dot(second, wzq1_ref[...])
    xs_ref[...] = dot(first, wxs0_ref[...]) + dot(second, wxs1_ref[...])
    wide0 = wide0_ref[:, :shard, :].reshape(half, wide0_ref.shape[2])
    wide1 = wide1_ref[:, :shard, :].reshape(half, wide1_ref.shape[2])
    wsk = (dot(to_g_ref[:, :half], wide0) + dot(to_g_ref[:, half:], wide1)).astype(bf16)
    wsk_ref[...] = wsk
    sk_ref[...] = dot(nat, wsk)


def pack_kernel(left_ref, right_ref, other_left_ref, other_right_ref, out_ref):
    cut = right_ref.shape[1]
    out_ref[:, :cut] = dot_tn(left_ref[...], right_ref[...]).astype(bf16)
    out_ref[:, cut:] = dot_tn(other_left_ref[...], other_right_ref[...]).astype(bf16)


def back_project_kernel(
    zx_ref, query_ref, sk_ref, wzq0_ref, wzq1_ref, wxs0_ref, wxs1_ref, wsk_ref, to_d_ref, rows_ref,
    scale_ref, out_ref, gain_ref,
):
    half = wsk_ref.shape[0] // 2
    channels = wzq0_ref.shape[1] - query_ref.shape[1]
    zq = jnp.concatenate([zx_ref[:, :channels], query_ref[...]], axis=1)
    xs = zx_ref[:, channels:]
    total = dot_nt(sk_ref[...], wsk_ref[...])
    for at, wzq_ref, wxs_ref in ((0, wzq0_ref, wxs0_ref), (half, wzq1_ref, wxs1_ref)):
        part = (dot_nt(zq, wzq_ref[...]) + dot_nt(xs, wxs_ref[...])).astype(bf16)
        total = total + dot_nt(part, to_d_ref[:, at : at + half])
    out_ref[...] = total.astype(bf16)
    gain_ref[...] = jnp.sum(
        total * rows_ref[...].astype(f32) * scale_ref[...], axis=0, keepdims=True
    )


def pack(left, right, other_left, other_right):
    rows, width = left.shape
    total = right.shape[1] + other_right.shape[1]
    part = 256 if width % 256 == 0 else width
    whole = lambda item: pl.BlockSpec(item.shape, lambda at: (0, 0))
    some = pl.BlockSpec((rows, part), lambda at: (0, at))
    return pl.pallas_call(
        pack_kernel,
        grid=(width // part,),
        in_specs=[some, whole(right), some, whole(other_right)],
        out_specs=pl.BlockSpec((part, total), lambda at: (at, 0)),
        out_shape=shape(bf16, width, total),
        cost_estimate=pl.CostEstimate(
            flops=2 * rows * width * total, bytes_accessed=2 * width * total, transcendentals=0
        ),
        compiler_params=pltpu.CompilerParams(vmem_limit_bytes=24 << 20),
    )(left, right, other_left, other_right)


def call(kernel, outs, flops, *args, scalars=0):
    moved = sum(item.size * item.dtype.itemsize for item in args)
    listed = outs if isinstance(outs, tuple) else (outs,)
    moved += sum(item.size * item.dtype.itemsize for item in listed)
    return pl.pallas_call(
        kernel,
        out_shape=outs,
        in_specs=[
            pl.BlockSpec(memory_space=pltpu.SMEM if at < scalars else pltpu.VMEM)
            for at in range(len(args))
        ],
        cost_estimate=pl.CostEstimate(flops=flops, bytes_accessed=moved, transcendentals=0),
        compiler_params=pltpu.CompilerParams(vmem_limit_bytes=24 << 20),
    )(*args)


def shape(dtype, *dims):
    return jax.ShapeDtypeStruct(dims, dtype)


class Ring:
    def __init__(self):
        self.count = lax.axis_size("dp")
        self.me = lax.axis_index("dp")
        bits = []
        bit = 2
        while bit < self.count:
            bits.append(bit)
            bit *= 2
        self.high_first = bits[::-1]
        self.orders = (bits, bits[::-1])

    def swap(self, value, bit):
        return lax.ppermute(value, "dp", [(i, i ^ bit) for i in range(self.count)])

    def rank_at(self, place):
        half = self.count // 2
        return self.me ^ ((place % half) * 2 + place // half)

    def gather(self, shard, kind):
        have = []
        value = shard
        lead = 0
        first = None
        for bit in self.orders[kind]:
            axis = sum(1 for other in have if other > bit)
            got = self.swap(value, bit)
            first = got if first is None else first
            value = jnp.stack([value, got], axis=axis)
            have.append(bit)
            lead += 1
        flat = (self.count // 2 * shard.shape[0],) + shard.shape[1:]
        return (value.reshape(flat), self.swap(value, 1).reshape(flat)), first

    def reduce(self, half_sum, kind):
        wire = half_sum.dtype
        levels = len(self.high_first)
        rest = (half_sum.shape[0] * 2 // self.count,) + half_sum.shape[1:]
        total = half_sum.astype(f32).reshape((2,) * levels + rest)
        left = list(self.high_first)
        for bit in self.orders[1 - kind]:
            axis = left.index(bit)
            keep = lax.index_in_dim(total, 0, axis, keepdims=False)
            send = lax.index_in_dim(total, 1, axis, keepdims=False).astype(wire)
            total = keep + self.swap(send, bit).astype(f32)
            left.remove(bit)
        return total


def turn(value, step):
    count = lax.axis_size("tensor")
    return lax.ppermute(value, "tensor", [(i, (i + step) % count) for i in range(count)])


def z_sum(value):
    total = value
    for step in range(1, lax.axis_size("tensor")):
        total = total + turn(value, step)
    return total


def z_scatter(value):
    count = lax.axis_size("tensor")
    rank = lax.axis_index("tensor")
    blocks = value.reshape((count, value.shape[0] // count) + value.shape[1:])

    def block(step):
        return lax.dynamic_index_in_dim(blocks, (rank + step) % count, 0, keepdims=False)

    got = [turn(block(step), step) for step in range(1, count)]
    total = block(0).astype(f32)
    for part in got:
        total = total + part.astype(f32)
    return total


def z_gather_async(value):
    count = lax.axis_size("tensor")
    rank = lax.axis_index("tensor")
    whole = jnp.zeros((count,) + value.shape, value.dtype)
    whole = lax.dynamic_update_index_in_dim(whole, value, rank, 0)
    for step in range(1, count):
        whole = lax.dynamic_update_index_in_dim(
            whole, turn(value, step), (rank - step) % count, 0
        )
    return whole.reshape((count * value.shape[0],) + value.shape[1:])


def z_gather(value):
    return lax.all_gather(value, "tensor", axis=0, tiled=True)


def local(
    block_input,
    positions,
    out_grad,
    in_gain,
    z_proj,
    x_proj,
    step_proj,
    state_proj,
    x_conv,
    x_conv_bias,
    state_conv,
    state_conv_bias,
    decay_log,
    step_bias,
    skip_gain,
    mixer_gain,
    mixer_out,
    query_proj,
    keyval_proj,
    attn_out,
    ffn_gain,
    gate_proj,
    up_proj,
    down_proj,
):
    ring = Ring()
    n = ring.count
    tensor = lax.axis_size("tensor")
    rank = lax.axis_index("tensor")
    width = block_input.shape[1]
    own_rows = block_input.shape[0]
    rows = own_rows * tensor
    heads = decay_log.shape[0]
    channels = heads * HD
    all_channels = channels * tensor
    shard = width // n
    piece = width // (n * tensor)
    kcount = x_conv.shape[0]
    q_local = query_proj.shape[1] // AHD
    group_size = q_local * tensor // KVH
    kv_head = rank * q_local // group_size
    state_width = 2 * NSTATE

    step_pad = (-heads) % 128
    inner = HD // n
    state_inner = state_width // (n * tensor)
    pack_width = state_width + keyval_proj.shape[1]
    shared_small = jnp.concatenate(
        [
            jnp.pad(jnp.stack([in_gain, ffn_gain]), ((0, kcount - 1), (0, 0))),
            jnp.concatenate([state_conv, state_conv_bias[None]], axis=0),
        ],
        axis=1,
    )
    shared_small = jnp.pad(
        shared_small, ((0, 15 - kcount), (0, pack_width - shared_small.shape[1]))
    )
    joined = jnp.concatenate(
        [jnp.concatenate([state_proj, keyval_proj], axis=1), shared_small], axis=0
    )
    own_small = jnp.concatenate([x_conv, x_conv_bias[None], mixer_gain[None]], axis=0)
    own_small = own_small.reshape(kcount + 2, heads * inner)
    joined = z_gather_async(joined).reshape(tensor, -1, pack_width)

    wzq, first_a = ring.gather(jnp.concatenate([z_proj, query_proj], axis=1), 0)
    wxs, first_b = ring.gather(
        jnp.concatenate([x_proj, jnp.pad(step_proj, ((0, 0), (0, step_pad)))], axis=1), 1
    )
    rows_nat = z_gather_async(block_input)
    shared = joined[:, :piece].reshape(shard, pack_width)
    small_at = state_width + 2 * AHD
    small_rows = joined[:, piece:]
    gain_cols = small_rows[:, :, :piece].transpose(1, 0, 2).reshape(16, -1)
    state_cols = small_rows[:, :, piece : piece + state_inner].transpose(1, 0, 2).reshape(16, -1)
    small_block = jnp.concatenate(
        [
            jnp.pad(own_small, ((0, 14 - kcount), (0, 128 - heads * inner))),
            jnp.pad(gain_cols, ((0, 0), (0, 128 - gain_cols.shape[1]))),
            jnp.pad(state_cols, ((0, 0), (0, small_at - 256 - state_cols.shape[1]))),
        ],
        axis=1,
    )
    wide = jnp.concatenate(
        [
            shared[:, :state_width],
            lax.dynamic_slice_in_dim(shared, state_width + kv_head * AHD, AHD, 1),
            lax.dynamic_slice_in_dim(shared, state_width + KVH * AHD + kv_head * AHD, AHD, 1),
        ],
        axis=1,
    )
    wide = jnp.concatenate([wide, small_block], axis=0)
    wide_parts, _ = ring.gather(wide, 1)
    wide_parts = [part.reshape(n // 2, -1, small_at) for part in wide_parts]

    late = lax.optimization_barrier((mixer_out, attn_out, gate_proj, up_proj, down_proj, wide))
    late = jnp.concatenate([late[0].T, late[1].T, late[2], late[3], late[4].T], axis=1)
    late_all = lax.all_gather(late, "dp", axis=0, tiled=True)
    cuts = [0]
    for item in (mixer_out.shape[0], attn_out.shape[0], gate_proj.shape[1], up_proj.shape[1], down_proj.shape[0]):
        cuts.append(cuts[-1] + item)
    w_mix, w_attn, w_gate, w_up, w_down = (
        late_all[:, cuts[i] : cuts[i + 1]] for i in range(5)
    )
    w_gu = late_all[:, cuts[2] : cuts[4]]
    ffl = gate_proj.shape[1]

    ranks = jnp.arange(n)
    pick = (ring.rank_at(ranks)[:, None] == ranks[None, :]).astype(f32)
    place = jnp.arange(width)
    feature_d = ring.rank_at(place // shard) * shard + place % shard
    inside = place % shard
    feature_g = (
        inside // piece * (width // tensor) + ring.rank_at(place // shard) * piece + inside % piece
    )
    to_d = (place[:, None] == feature_d[None, :]).astype(bf16)
    to_g = (place[:, None] == feature_g[None, :]).astype(bf16)
    half = width // 2
    own_resid = block_input.astype(f32)
    small_width = small_at
    (
        normed_nat, normed, normed_g, zq_lin, xs_lin, sk_lin, w_sk, in_scale, x_small, gains_all,
        state_small_in,
    ) = call(
        functools.partial(project_kernel, tensor),
        (
            shape(bf16, rows, width),
            shape(bf16, rows, width),
            shape(bf16, rows, width),
            shape(f32, rows, wzq[0].shape[1]),
            shape(f32, rows, wxs[0].shape[1]),
            shape(f32, rows, small_width),
            shape(bf16, width, small_width),
            shape(f32, rows, 1),
            shape(f32, 16, channels),
            shape(f32, 16, width),
            shape(f32, 16, state_width),
        ),
        4 * 10**9,
        ring.rank_at(ranks), rows_nat, *wzq, *wxs, *wide_parts, to_d, to_g,
        scalars=1,
    )
    in_gain_f, ffn_gain_f = gains_all[0], gains_all[1]
    mixer_gain_f = x_small[kcount + 1]
    grad_all = z_gather_async(lax.optimization_barrier((out_grad, rows_nat))[0])
    position = positions.reshape(rows, 1)
    decay_rate = -jnp.exp(decay_log)
    lanes_pad = (0, step_pad)
    head_rows = jnp.stack([jnp.pad(step_bias, lanes_pad), jnp.pad(decay_rate, lanes_pad)])
    skip_row = jnp.repeat(skip_gain, HD)[None]
    step_width = heads + step_pad
    ssm_params = (position, x_small, state_small_in, head_rows, skip_row)
    gated_out = call(
        functools.partial(ssm_forward_kernel, kcount),
        shape(f32, rows, channels),
        2 * 10**9,
        zq_lin, xs_lin, sk_lin, *ssm_params,
    )
    square_sums = z_sum(jnp.sum(gated_out * gated_out, axis=1))
    freq_rates = rope_base ** (-2.0 * jnp.arange(AHD // 2, dtype=f32) / AHD)
    angles = positions.astype(f32)[:, None] * freq_rates[None, :]
    cosine, sine = jnp.cos(angles), jnp.sin(angles)
    cosine = jnp.concatenate([cosine, cosine], axis=1)
    sine = jnp.concatenate([-sine, sine], axis=1)
    context = call(
        attention_forward_kernel,
        shape(bf16, rows, q_local * AHD),
        2 * 10**9,
        zq_lin, sk_lin, position, cosine, sine,
    )
    ssm_scale = lax.rsqrt(square_sums / all_channels + norm_eps)[:, None]
    ssm_normed = (gated_out * ssm_scale * mixer_gain_f[None, :]).astype(bf16)

    mixed = z_scatter((dot_nt(ssm_normed, w_mix) + dot_nt(context, w_attn)).astype(bf16))
    hidden = own_resid + mixed
    ff_scale = lax.rsqrt(jnp.mean(hidden * hidden, axis=1, keepdims=True) + norm_eps)
    ffn_in = z_gather((hidden * ff_scale * ffn_gain_f[None, :]).astype(bf16))

    gu_lin = dot(ffn_in, w_gu)
    gate_lin, up_lin = gu_lin[:, :ffl], gu_lin[:, ffl:]
    gate_act = jax.nn.silu(gate_lin)
    ffn_act = (gate_act * up_lin).astype(bf16)
    act_grad = dot(grad_all, w_down)
    gate_back = (act_grad * up_lin * silu_grad(gate_lin)).astype(bf16)
    up_back = (act_grad * gate_act).astype(bf16)
    gu_back = jnp.concatenate([gate_back, up_back], axis=1)
    ffn_pack = pack(ffn_in, gu_back, grad_all, ffn_act)
    ffn_back = z_scatter(dot_nt(gu_back, w_gu).astype(bf16))
    ffn_back, ffn_pack = lax.optimization_barrier((ffn_back, ffn_pack))
    ffn_gain_part = jnp.sum(ffn_back * hidden * ff_scale, axis=0)
    ffn_norm_back = ffn_back * ffn_gain_f[None, :]
    resid_grad = (
        out_grad.astype(f32)
        + ff_scale * ffn_norm_back
        - hidden * ff_scale**3 * jnp.mean(ffn_norm_back * hidden, axis=1, keepdims=True)
    )
    resid_all = z_gather(resid_grad.astype(bf16))
    ffn_red = lax.psum_scatter(ffn_pack, "dp", scatter_dimension=0, tiled=True).astype(f32)

    ssm_back = dot(resid_all, w_mix)
    ctx_back = dot(resid_all, w_attn)
    row_dots = z_sum(jnp.sum(ssm_back * mixer_gain_f[None, :] * gated_out, axis=1))
    query_grad, kv_grad = call(
        attention_backward_kernel,
        (shape(bf16, rows, q_local * AHD), shape(bf16, rows, 2 * AHD)),
        2 * 10**9,
        zq_lin, sk_lin, position, cosine, sine, ctx_back,
    )
    mid_pack = pack(
        resid_all, jnp.concatenate([ssm_normed, context], axis=1), normed_nat, query_grad
    )
    row_dots, mid_pack, ffn_red = lax.optimization_barrier((row_dots, mid_pack, ffn_red))
    mid_red = lax.psum_scatter(mid_pack, "dp", scatter_dimension=0, tiled=True).astype(f32)
    qwide = q_local * AHD
    mixer_red = mid_red[:, :channels].T
    attn_red = mid_red[:, channels : channels + qwide].T
    query_red = mid_red[:, channels + qwide :]
    ffn_rows = z_scatter(
        lax.optimization_barrier((dot_nt(ffn_act, w_down).astype(bf16), row_dots))[0]
    )
    output = (hidden + ffn_rows).astype(bf16)
    pull = ssm_scale**3 * row_dots[:, None] / all_channels
    zx_half, state_half, wide_sums, state_sums, lane_sums = call(
        functools.partial(ssm_backward_kernel, kcount),
        (
            shape(bf16, rows, 2 * channels + step_width),
            shape(bf16, rows, state_width),
            shape(f32, kcount + 4, channels),
            shape(f32, kcount + 4, state_width),
            shape(f32, 8, step_width),
        ),
        4 * 10**9,
        ssm_back, gated_out, jnp.concatenate([ssm_scale, pull], axis=1),
        zq_lin, xs_lin, sk_lin, *ssm_params,
    )
    x_taps_grad = wide_sums[:kcount]
    x_bias_grad = wide_sums[kcount]
    mixer_gain_grad = wide_sums[kcount + 1]
    skip_grad = jnp.sum(wide_sums[kcount + 2].reshape(heads, HD), axis=1)
    step_bias_grad = lane_sums[0, :heads]
    decay_log_grad = lane_sums[1, :heads]
    sk_half = jnp.concatenate([state_half, kv_grad], axis=1)
    zx_send = dot_tn(normed[:, half:], zx_half).astype(bf16)
    sk_send = dot_tn(normed_g[:, half:], sk_half).astype(bf16)
    zx_sum = dot_tn(normed[:, :half], zx_half) + ring.swap(zx_send, 1).astype(f32)
    sk_sum = dot_tn(normed_g[:, :half], sk_half) + ring.swap(sk_send, 1).astype(f32)
    zx_in, sk_in, zx_sum, sk_sum = lax.optimization_barrier(
        (zx_half, sk_half, zx_sum.astype(bf16), sk_sum.astype(bf16))
    )
    normed_back, in_gain_sum = call(
        back_project_kernel,
        (shape(bf16, rows, width), shape(f32, 1, width)),
        3 * 10**9,
        zx_in, query_grad, sk_in, *wzq, *wxs, w_sk, to_d, rows_nat, in_scale,
    )
    zx_red = ring.reduce(zx_sum, 1)
    sk_red = ring.reduce(sk_sum, 0)
    normed_back_own = z_scatter(normed_back)
    gate_red = ffn_red[:, :ffl]
    up_red = ffn_red[:, ffl : 2 * ffl]
    down_red = ffn_red[:, 2 * ffl :].T
    z_red = zx_red[:, :channels]
    xs_red = zx_red[:, channels:]

    own_in_scale = lax.rsqrt(jnp.mean(own_resid * own_resid, axis=1, keepdims=True) + norm_eps)
    gains = jnp.stack([in_gain_sum[0], ffn_gain_part])

    def by_rank(value):
        lead = value.size // HD
        return value.reshape(lead, n, inner).transpose(1, 0, 2).reshape(n, lead * inner)

    head_terms = jnp.concatenate([decay_log_grad, step_bias_grad, skip_grad])
    state_small = state_sums[: kcount + 1]
    per_rank = [
        by_rank(x_taps_grad),
        by_rank(x_bias_grad),
        by_rank(mixer_gain_grad),
        jnp.broadcast_to(head_terms[None], (n, 3 * heads)),
    ]
    per_both = jnp.concatenate(
        [
            gains.reshape(2, tensor, n, piece).transpose(2, 1, 0, 3).reshape(n, tensor, -1),
            state_small.reshape(kcount + 1, tensor, n, state_inner)
            .transpose(2, 1, 0, 3)
            .reshape(n, tensor, -1),
        ],
        axis=2,
    )
    both_size = per_both.shape[2]
    flat = jnp.concatenate(per_rank + [per_both.reshape(n, -1)], axis=1)
    flat = jnp.dot(pick, flat, precision=HIGHEST)
    flat_red = ring.reduce(flat[: n // 2] + ring.swap(flat[n // 2 :], 1), 0)[0]
    parts = []
    at = 0
    for item in per_rank:
        parts.append(flat_red[at : at + item.shape[1]])
        at += item.shape[1]
    x_taps_red = parts[0].reshape(kcount, heads, inner)
    x_bias_red = parts[1].reshape(heads, inner)
    mixer_gain_red = parts[2].reshape(heads, inner)
    heads_red = parts[3].reshape(3, heads)
    sk_blocks = sk_red.astype(bf16).reshape(tensor, piece, -1)
    both_rows = flat_red[at:].astype(bf16).reshape(tensor, 1, both_size)
    both_rows = jnp.pad(both_rows, ((0, 0), (0, 15), (0, sk_blocks.shape[2] - both_size)))
    sk_blocks = jnp.concatenate([sk_blocks, both_rows], axis=1)
    both_red = jnp.zeros((both_size,), f32)
    state_own = jnp.zeros((piece, state_width), f32)
    key_cols = [jnp.zeros((piece, AHD), f32) for _ in range(KVH)]
    value_cols = [jnp.zeros((piece, AHD), f32) for _ in range(KVH)]
    for step in range(tensor):
        sent = lax.dynamic_index_in_dim(sk_blocks, (rank + step) % tensor, 0, keepdims=False)
        got = (turn(sent, step) if step else sent).astype(f32)
        both_red = both_red + got[piece, :both_size]
        got = got[:piece]
        head_of = (rank - step) % tensor * q_local // group_size
        state_own = state_own + got[:, :state_width]
        for head in range(KVH):
            term = jnp.where(head_of == head, got[:, state_width:], 0.0)
            key_cols[head] = key_cols[head] + term[:, :AHD]
            value_cols[head] = value_cols[head] + term[:, AHD:]
    keyval_red = jnp.concatenate(key_cols + value_cols, axis=1)
    in_gain_red = both_red[:piece]
    ffn_gain_red = both_red[piece : 2 * piece]
    state_small_red = both_red[2 * piece :].reshape(kcount + 1, state_inner)

    in_back = normed_back_own * in_gain_f[None, :]
    input_grad = (
        resid_grad
        + own_in_scale * in_back
        - own_resid * own_in_scale**3 * jnp.mean(in_back * own_resid, axis=1, keepdims=True)
    )
    return (
        output,
        input_grad,
        in_gain_red,
        z_red,
        xs_red[:, :channels],
        xs_red[:, channels : channels + heads],
        state_own,
        x_taps_red,
        x_bias_red,
        state_small_red[:kcount],
        state_small_red[kcount],
        heads_red[0],
        heads_red[1],
        heads_red[2],
        mixer_gain_red,
        mixer_red,
        query_red,
        keyval_red,
        attn_red,
        ffn_gain_red,
        gate_red,
        up_red,
        down_red,
    )


def solution(mesh):
    in_specs = (
        P(("dp", "tensor"), None),
        P("dp"),
        P(("dp", "tensor"), None),
        P(("tensor", "dp")),
        P("dp", "tensor"),
        P("dp", "tensor"),
        P("dp", "tensor"),
        P(("tensor", "dp"), None),
        P(None, "tensor", "dp"),
        P("tensor", "dp"),
        P(None, ("tensor", "dp")),
        P(("tensor", "dp")),
        P("tensor"),
        P("tensor"),
        P("tensor"),
        P("tensor", "dp"),
        P("tensor", "dp"),
        P("dp", "tensor"),
        P(("tensor", "dp"), None),
        P("tensor", "dp"),
        P(("tensor", "dp")),
        P("dp", "tensor"),
        P("dp", "tensor"),
        P("tensor", "dp"),
    )
    out_specs = (
        P(("dp", "tensor"), None),
        P(("dp", "tensor"), None),
        P(("tensor", "dp")),
        P("dp", "tensor"),
        P("dp", "tensor"),
        P("dp", "tensor"),
        P(("tensor", "dp"), None),
        P(None, "tensor", "dp"),
        P("tensor", "dp"),
        P(None, ("tensor", "dp")),
        P(("tensor", "dp")),
        P("tensor"),
        P("tensor"),
        P("tensor"),
        P("tensor", "dp"),
        P("tensor", "dp"),
        P("dp", "tensor"),
        P(("tensor", "dp"), None),
        P("tensor", "dp"),
        P(("tensor", "dp")),
        P("dp", "tensor"),
        P("dp", "tensor"),
        P("tensor", "dp"),
    )
    return jax.shard_map(local, mesh=mesh, in_specs=in_specs, out_specs=out_specs, check_vma=False)
```
